256 devices in a mesh: seq: 32 (over z_hi, x, y), head: 8 (over z_lo, core).
Axes of the slice: x: 4, y: 4, z: 8 (z_hi: 2, z_lo: 4; z = z_hi * 4 + z_lo), core: 2. Of those that a mesh axis runs over, the one named last changes fastest.
Arguments:
- queries: bfloat16 [8192, 64, 192], P('seq', 'head'), may hold values from -50 to 50
- grad_out: bfloat16 [8192, 64, 128], P('seq', 'head'), may hold values from -6 to 6
- latent: bfloat16 [8192, 576], P('seq'), may hold values from -18 to 18
- w_uk: bfloat16 [64, 512, 128], P('head'), may hold values from -0.25 to 0.25
- w_uv: bfloat16 [64, 512, 128], P('head'), may hold values from -0.25 to 0.25
- doc_start: int32 [8192], P('seq'), may hold values from 0 to 8191, as said below
Outputs:
- grad_query: bfloat16 [8192, 64, 192], P('seq', 'head')
- grad_latent: float32 [8192, 576], P(('seq', 'head'))
The draws below stay inside these ranges and needn't reach their ends.
Inputs may be any that keep to these rules, and one draw needn't show every extreme that they name: doc_start[t] is the first position of the document that holds position t; documents follow one another, each of 1 to 768 positions, and one is exactly 768 long.
All inputs are finite; a program needn't handle non-finite values.
Results may differ from the reference program's by a relative error of at most 0.008.
Values may be sent and summed in bfloat16 or wider, within the bound.
No kernel may reach another device: no remote copies, remote signals or barrier semaphores. Data moves between devices by JAX's collectives and lax.ppermute only.
A program may use at most 64 MiB of HBM per device.

```python
import jax
import jax.numpy as jnp
from jax import lax

HEADS = 64
NOPE = 128
ROPE = 64
LATENT = 512
VDIM = 128
T_DEV = 256
BACK = 3
MOST = 768
SEQ = 8192
N_SEQ = 32


def draw_latent(key, part):
    values = jnp.clip(jax.random.normal(jax.random.fold_in(key, 11), (SEQ, LATENT + ROPE), jnp.float32), -6.0, 6.0)
    return values.astype(jnp.bfloat16)


def draw_queries(key, part):
    values = jnp.clip(jax.random.normal(jax.random.fold_in(key, 21), (SEQ, HEADS, NOPE + ROPE), jnp.float32), -6.0, 6.0)
    return values.astype(jnp.bfloat16)


def draw_doc_start(key, part):
    key_len, key_first = jax.random.split(jax.random.fold_in(key, 31))
    lengths = jax.random.randint(key_len, (SEQ,), 1, MOST + 1)
    first = jax.random.randint(key_first, (), 1, T_DEV)
    lengths = lengths.at[0].set(first).at[1].set(MOST)
    ends = jnp.cumsum(lengths).astype(jnp.int32)
    starts = (ends - lengths).astype(jnp.int32)
    position = jnp.arange(SEQ, dtype=jnp.int32)
    which = jnp.searchsorted(ends, position, side='right')
    result = starts[which].astype(jnp.int32)
    result = jnp.where(position == SEQ - 1, SEQ - 1, result)
    return result.astype(jnp.int32)


def block_levels(own_key, shape, shards, least, top_value):
    factor_of = 1.0
    for dim, blocks in shards:
        draws = jax.random.uniform(jax.random.fold_in(jax.random.fold_in(own_key, 6), dim), (blocks,), jnp.float32, least / len(shards), top_value / len(shards))
        factor_of = factor_of * jnp.repeat(jnp.exp(draws), shape[dim] // blocks).reshape((-1,) + (1,) * (len(shape) - 1 - dim))
    return factor_of


def normal_values(stream_key, dims, scale, most, cuts=(), kind=jnp.bfloat16):
    drawn = jax.random.normal(stream_key, dims, jnp.float32) * scale
    if len(cuts) > 0:
        drawn = block_levels(stream_key, dims, cuts, -0.22, 0.18) * drawn
    return jnp.clip(drawn, min=-most, max=most).astype(kind)


def setup_inputs(seed: int = 0) -> dict:
    splits = jax.random.split(jax.random.key(seed), 7)
    queries = draw_queries(jax.random.fold_in(splits[6], 71), 0)
    grad_out = normal_values(splits[1], (SEQ, HEADS, VDIM), 1.0, 6.0, ((0, 32), (1, 8)))
    latent = draw_latent(jax.random.fold_in(splits[6], 71), 0)
    w_uk = normal_values(splits[3], (HEADS, LATENT, NOPE), LATENT ** -0.5, 0.25, ((0, 8),))
    w_uv = normal_values(splits[4], (HEADS, LATENT, VDIM), LATENT ** -0.5, 0.25, ((0, 8),))
    doc_start = draw_doc_start(jax.random.fold_in(splits[6], 71), 0)
    return dict(queries=queries, grad_out=grad_out, latent=latent, w_uk=w_uk, w_uv=w_uv, doc_start=doc_start)


def rounded(values):
    return lax.optimization_barrier(values.astype(jnp.bfloat16)).astype(jnp.float32)


def reference(queries, grad_out, latent, w_uk, w_uv, doc_start):
    width = LATENT + ROPE
    factor = (NOPE + ROPE) ** -0.5
    span = (BACK + 1) * T_DEV
    front = BACK * T_DEV
    padded = jnp.concatenate([jnp.zeros((front, width), latent.dtype), latent], 0)
    uk_full = w_uk.astype(jnp.float32)
    uv_full = w_uv.astype(jnp.float32)

    def step(carry, index):
        start = (index * T_DEV).astype(jnp.int32)
        query = lax.dynamic_slice_in_dim(queries, start, T_DEV, 0).astype(jnp.float32)
        cotangent = lax.dynamic_slice_in_dim(grad_out, start, T_DEV, 0).astype(jnp.float32)
        starts = lax.dynamic_slice_in_dim(doc_start, start, T_DEV, 0)
        keys = lax.dynamic_slice_in_dim(padded, start, span, 0).astype(jnp.float32)
        qpos = start + jnp.arange(T_DEV, dtype=jnp.int32)
        kpos = start - front + jnp.arange(span, dtype=jnp.int32)
        visible = (kpos[None, :] >= starts[:, None]) & (kpos[None, :] <= qpos[:, None])
        q_abs = rounded(jnp.einsum('thn,hln->thl', query[:, :, :NOPE], uk_full))
        qcat = jnp.concatenate([q_abs, query[:, :, NOPE:]], -1)
        scores = jnp.einsum('thc,uc->htu', qcat, keys) * factor
        scores = jnp.where(visible[None], scores, -jnp.inf)
        top = jnp.max(scores, -1, keepdims=True)
        expo = jnp.exp(scores - top)
        probs = rounded(expo / jnp.sum(expo, -1, keepdims=True))
        grad_lat = rounded(jnp.einsum('thv,hlv->thl', cotangent, uv_full))
        o_lat = jnp.einsum('htu,ul->thl', probs, keys[:, :LATENT])
        delta = jnp.sum(grad_lat * o_lat, -1)
        dprob = jnp.einsum('thl,ul->htu', grad_lat, keys[:, :LATENT])
        dscore = rounded(probs * (dprob - delta.T[:, :, None]))
        dq_cat = jnp.einsum('htu,uc->thc', dscore, keys) * factor
        dq_nope = jnp.einsum('thl,hln->thn', rounded(dq_cat[:, :, :LATENT]), uk_full)
        grad_query = jnp.concatenate([dq_nope, dq_cat[:, :, LATENT:]], -1).astype(jnp.bfloat16)
        dkey = jnp.einsum('htu,thc->uc', dscore, qcat) * factor
        dvalue = jnp.einsum('htu,thl->ul', probs, grad_lat)
        dkey = dkey + jnp.pad(dvalue, ((0, 0), (0, ROPE)))
        window = lax.dynamic_slice_in_dim(carry, start, span, 0) + dkey
        carry = lax.dynamic_update_slice_in_dim(carry, window, start, 0)
        return carry, grad_query

    init = jnp.zeros((front + N_SEQ * T_DEV, width), jnp.float32)
    total, pieces = lax.scan(step, init, jnp.arange(N_SEQ, dtype=jnp.int32))
    return pieces.reshape(N_SEQ * T_DEV, HEADS, NOPE + ROPE), total[front:]
```

```python
import functools
import math

import jax
import jax.numpy as jnp
from jax import lax
from jax.experimental import pallas as pl
from jax.experimental.pallas import tpu as pltpu
from jax.sharding import PartitionSpec as P

BACK = 3
CORES = 2
BF16 = jnp.bfloat16
F32 = jnp.float32


def dot(a, b, contract=((1,), (0,))):
    return lax.dot_general(a, b, (contract, ((), ())), preferred_element_type=F32)


def prepare_kernel(
    first_ref, q_ref, qt_ref, g_ref, gt_ref, uk_ref, uv_ref, start_ref,
    qct_ref, qc_ref, glt_ref, gl_ref, bias_ref,
):
    latw, nope = uk_ref.shape[1:]
    uk, uv = uk_ref[0], uv_ref[0]
    qct_ref[0, :latw] = dot(uk, qt_ref[0, :nope]).astype(BF16)
    qct_ref[0, latw:] = qt_ref[0, nope:]
    qc_ref[:, :latw] = dot(q_ref[0, :, :nope], uk, ((1,), (1,))).astype(BF16)
    qc_ref[:, latw:] = q_ref[0, :, nope:]
    glt_ref[0] = dot(uv, gt_ref[0]).astype(BF16)
    gl_ref[...] = dot(g_ref[0], uv, ((1,), (1,))).astype(BF16)
    shape = bias_ref.shape
    tokens = shape[1]
    row = pl.program_id(0) * shape[0] + lax.broadcasted_iota(jnp.int32, shape, 0)
    kpos = first_ref[0] + row
    qpos = first_ref[0] + BACK * tokens + lax.broadcasted_iota(jnp.int32, shape, 1)
    visible = (kpos >= start_ref[...]) & (kpos <= qpos)
    bias_ref[...] = jnp.where(visible, 0.0, -jnp.inf).astype(F32)


def prepare(first, q, qt, g, gt, w_uk, w_uv, doc_start):
    heads, tokens, qw = q.shape
    latw, nope = w_uk.shape[1:]
    vdim = g.shape[2]
    width = latw + qw - nope
    span = (BACK + 1) * tokens
    one = lambda *dims: pl.BlockSpec((1, *dims), lambda h, s: (h, 0, 0))
    rows = lambda n, d: pl.BlockSpec((n, d), lambda h, s: (h, 0))
    return pl.pallas_call(
        prepare_kernel,
        out_shape=(
            jax.ShapeDtypeStruct((heads, width, tokens), BF16),
            jax.ShapeDtypeStruct((heads * tokens, width), BF16),
            jax.ShapeDtypeStruct((heads, latw, tokens), BF16),
            jax.ShapeDtypeStruct((heads * tokens, latw), BF16),
            jax.ShapeDtypeStruct((span, tokens), F32),
        ),
        grid_spec=pltpu.PrefetchScalarGridSpec(
            num_scalar_prefetch=1,
            grid=(heads,),
            in_specs=[
                one(tokens, qw), one(qw, tokens), one(tokens, vdim), one(vdim, tokens),
                one(latw, nope), one(latw, vdim),
                pl.BlockSpec((1, tokens), lambda h, s: (0, 0)),
            ],
            out_specs=[
                one(width, tokens), rows(tokens, width), one(latw, tokens),
                rows(tokens, latw), rows(span // heads, tokens),
            ],
        ),
        cost_estimate=pl.CostEstimate(
            flops=8 * heads * tokens * latw * nope, transcendentals=0,
            bytes_accessed=16 << 20,
        ),
        name="prepare",
    )(first, q, qt, g, gt, w_uk, w_uv, doc_start)


def main_kernel(
    info_ref, qct_ref, glt_ref, bias_ref, own_ref,
    m3_ref, m2_ref, m1_ref, t3_ref, t2_ref, t1_ref, qc_hbm, gl_hbm,
    ds_ref, keep_ref, send_ref,
    keys_s, score_s, dprob_s, p_s, ds_s, qc_s, gl_s, sems, *, factor,
):
    head = pl.program_id(0)
    core, low = info_ref[0], info_ref[1]
    span, tokens = bias_ref.shape
    latw = glt_ref.shape[1]
    half = tokens // CORES
    chunk = 128
    chunks = span // chunk
    scale = factor * math.log2(math.e)
    lane = pl.ds(pl.multiple_of(head * tokens, tokens), tokens)

    @pl.when(head == 0)
    def _():
        pltpu.make_async_copy(qc_hbm, qc_s, sems.at[0]).start()
        pltpu.make_async_copy(gl_hbm, gl_s, sems.at[1]).start()
        for block, (mine, theirs) in enumerate(
            ((m3_ref, t3_ref), (m2_ref, t2_ref), (m1_ref, t1_ref))
        ):
            keys_s[pl.ds(pl.multiple_of(block * tokens + core * half, half), half)] = mine[...]
            keys_s[pl.ds(pl.multiple_of(block * tokens + (1 - core) * half, half), half)] = theirs[...]
        keys_s[BACK * tokens :] = own_ref[...]

    def at(c):
        return pl.ds(pl.multiple_of(c * chunk, chunk), chunk)

    def fold(x, op):
        return op(x.reshape(chunk // 8, 8, tokens), axis=0)

    def score(c, top):
        s = dot(keys_s[at(c)], qct_ref[0]) * scale + bias_ref[at(c)]
        score_s[at(c)] = s
        return jnp.maximum(top, fold(s, jnp.max))

    top = lax.fori_loop(low, chunks, score, jnp.full((8, tokens), -jnp.inf, F32))
    top = jnp.max(top, axis=0, keepdims=True)

    def expo(c, total):
        e = jnp.exp2(score_s[at(c)] - top)
        score_s[at(c)] = e
        return total + fold(e, jnp.sum)

    total = lax.fori_loop(low, chunks, expo, jnp.zeros((8, tokens), F32))
    inverse = 1.0 / jnp.sum(total, axis=0, keepdims=True)

    def prob(c, delta):
        p = (score_s[at(c)] * inverse).astype(BF16)
        dp = dot(keys_s[at(c), :latw], glt_ref[0])
        p_s[at(c), lane] = p
        dprob_s[at(c)] = dp
        return delta + fold(p.astype(F32) * dp, jnp.sum)

    delta = lax.fori_loop(low, chunks, prob, jnp.zeros((8, tokens), F32))
    delta = jnp.sum(delta, axis=0, keepdims=True)

    def dscore(c, _):
        ds = (p_s[at(c), lane].astype(F32) * (dprob_s[at(c)] - delta)).astype(BF16)
        ds_s[at(c), lane] = ds
        ds_ref[0, at(c)] = ds
        return 0

    lax.fori_loop(low, chunks, dscore, 0)

    def blank(c, _):
        zero = jnp.zeros((chunk, tokens), BF16)
        p_s[at(c), lane] = zero
        ds_s[at(c), lane] = zero
        ds_ref[0, at(c)] = zero
        return 0

    lax.fori_loop(0, low, blank, 0)

    @pl.when(head == pl.num_programs(0) - 1)
    def _():
        pltpu.make_async_copy(qc_hbm, qc_s, sems.at[0]).wait()
        pltpu.make_async_copy(gl_hbm, gl_s, sems.at[1]).wait()
        piece = keep_ref.shape[2]
        groups = keep_ref.shape[1]

        def gradient(block, side):
            rows = [
                pl.ds(pl.multiple_of(block * tokens + (g * CORES + side) * piece, piece), piece)
                for g in range(groups)
            ]
            ds = jnp.concatenate([ds_s[r] for r in rows], 0)
            p = jnp.concatenate([p_s[r] for r in rows], 0)
            key = dot(ds, qc_s[...]) * factor
            value = dot(p, gl_s[...])
            return key[:, :latw] + value, key[:, latw:]

        def each(block, _):
            mine_value, mine_rope = gradient(block, core)
            keep_ref[block, :, :, :latw] = mine_value.reshape(groups, piece, -1)
            keep_ref[block, :, :, latw:] = mine_rope.reshape(groups, piece, -1)
            value, rope = gradient(block, 1 - core)
            send_ref[block, :, :, :latw] = value.astype(BF16).reshape(groups, piece, -1)
            send_ref[block, :, :, latw:] = rope.astype(BF16).reshape(groups, piece, -1)
            return 0

        lax.fori_loop(0, BACK + 1, each, 0)


def attend(info, qct, glt, bias, own, mine, theirs, qc, gl, factor, groups):
    heads, width, tokens = qct.shape
    latw = glt.shape[1]
    span = bias.shape[0]
    piece = tokens // CORES // groups
    head = lambda d: pl.BlockSpec((1, d, tokens), lambda h, s: (h, 0, 0))
    whole = lambda a: pl.BlockSpec(a.shape, lambda h, s: (0,) * a.ndim)
    out = (BACK + 1, groups, piece, width)
    return pl.pallas_call(
        functools.partial(main_kernel, factor=factor),
        out_shape=(
            jax.ShapeDtypeStruct((heads, span, tokens), BF16),
            jax.ShapeDtypeStruct(out, F32),
            jax.ShapeDtypeStruct(out, BF16),
        ),
        grid_spec=pltpu.PrefetchScalarGridSpec(
            num_scalar_prefetch=1,
            grid=(heads,),
            in_specs=[head(width), head(latw), whole(bias), whole(own)]
            + [whole(a) for a in (*mine, *theirs)]
            + [pl.BlockSpec(memory_space=pl.ANY)] * 2,
            out_specs=[
                pl.BlockSpec((1, span, tokens), lambda h, s: (h, 0, 0)),
                pl.BlockSpec(out, lambda h, s: (0, 0, 0, 0)),
                pl.BlockSpec(out, lambda h, s: (0, 0, 0, 0)),
            ],
            scratch_shapes=[
                pltpu.VMEM((span, width), BF16),
                pltpu.VMEM((span, tokens), F32),
                pltpu.VMEM((span, tokens), F32),
                pltpu.VMEM((span, heads * tokens), BF16),
                pltpu.VMEM((span, heads * tokens), BF16),
                pltpu.VMEM(qc.shape, BF16),
                pltpu.VMEM(gl.shape, BF16),
                pltpu.SemaphoreType.DMA((2,)),
            ],
        ),
        compiler_params=pltpu.CompilerParams(vmem_limit_bytes=56 << 20),
        cost_estimate=pl.CostEstimate(
            flops=2 * heads * tokens * span * (2 * width + 2 * latw),
            transcendentals=heads * tokens * span, bytes_accessed=24 << 20,
        ),
        name="attend",
    )(info, qct, glt, bias, own, *mine, *theirs, qc, gl)


def query_kernel(
    info_ref, ds_ref, ukt_ref, own_ref, m3_ref, m2_ref, m1_ref, t3_ref, t2_ref, t1_ref,
    out_ref, keys_s, *, factor,
):
    core = info_ref[0]
    tokens, width = own_ref.shape
    half = tokens // CORES
    nope, latw = ukt_ref.shape[1:]

    @pl.when(pl.program_id(0) == 0)
    def _():
        for block, (mine, theirs) in enumerate(
            ((m3_ref, t3_ref), (m2_ref, t2_ref), (m1_ref, t1_ref))
        ):
            keys_s[:, pl.ds(pl.multiple_of(block * tokens + core * half, half), half)] = mine[...].T
            keys_s[:, pl.ds(pl.multiple_of(block * tokens + (1 - core) * half, half), half)] = theirs[...].T
        keys_s[:, BACK * tokens :] = own_ref[...].T

    dq = dot(keys_s[...], ds_ref[0]) * factor
    dq_nope = dot(ukt_ref[0], dq[:latw].astype(BF16))
    out_ref[0, :, :nope] = dq_nope.T.astype(BF16)
    out_ref[0, :, nope:] = dq[latw:].T.astype(BF16)


def query_gradient(info, ds, ukt, own, mine, theirs, factor):
    heads, span, tokens = ds.shape
    nope, latw = ukt.shape[1:]
    width = own.shape[1]
    qw = nope + width - latw
    whole = lambda a: pl.BlockSpec(a.shape, lambda h, s: (0,) * a.ndim)
    return pl.pallas_call(
        functools.partial(query_kernel, factor=factor),
        out_shape=jax.ShapeDtypeStruct((heads, tokens, qw), BF16),
        grid_spec=pltpu.PrefetchScalarGridSpec(
            num_scalar_prefetch=1,
            grid=(heads,),
            in_specs=[
                pl.BlockSpec((1, span, tokens), lambda h, s: (h, 0, 0)),
                pl.BlockSpec((1, nope, latw), lambda h, s: (h, 0, 0)),
                whole(own),
            ]
            + [whole(a) for a in (*mine, *theirs)],
            out_specs=pl.BlockSpec((1, tokens, qw), lambda h, s: (h, 0, 0)),
            scratch_shapes=[pltpu.VMEM((width, span), BF16)],
        ),
        compiler_params=pltpu.CompilerParams(vmem_limit_bytes=32 << 20),
        cost_estimate=pl.CostEstimate(
            flops=2 * heads * tokens * (span * width + latw * nope),
            transcendentals=0, bytes_accessed=8 << 20,
        ),
        name="query_gradient",
    )(info, ds, ukt, own, *mine, *theirs)


def along_seq(distance):
    devices, heads = lax.axis_size("seq"), lax.axis_size("head")
    pairs = []
    for source in range(devices):
        target = source + distance
        if not 0 <= target < devices:
            continue
        crossing = (2 * source < devices) != (2 * target < devices)
        for head in range(heads):
            chip, core = divmod(head, CORES)
            if crossing:
                chip = heads // CORES - 1 - chip
            pairs.append((source * heads + head, target * heads + chip * CORES + core))
    return pairs


def move(value, distance):
    return lax.ppermute(value, ("seq", "head"), along_seq(distance))


def swap_cores(value):
    return lax.ppermute(value, "head", [(k, k ^ 1) for k in range(lax.axis_size("head"))])


def shards(queries, grad_out, latent, w_uk, w_uv, doc_start):
    tokens, width = latent.shape
    factor = queries.shape[2] ** (-0.5)
    seq, head = lax.axis_index("seq"), lax.axis_index("head")
    heads = lax.axis_size("head")
    chips = heads // CORES
    core, chip = head % CORES, head // CORES
    half = tokens // CORES

    part = lax.dynamic_slice_in_dim(latent, core * half, half, 0)
    mine = [move(part, distance) for distance in range(BACK, 0, -1)]
    theirs = [swap_cores(piece) for piece in mine]

    first = (seq - BACK) * tokens
    low = jnp.maximum(doc_start[0] - first, 0) // 128
    info = jnp.stack([core, low]).astype(jnp.int32)
    q = jnp.transpose(queries, (1, 0, 2))
    qt = jnp.transpose(queries, (1, 2, 0))
    g = jnp.transpose(grad_out, (1, 0, 2))
    gt = jnp.transpose(grad_out, (1, 2, 0))
    ukt = jnp.transpose(w_uk, (0, 2, 1))
    qct, qc, glt, gl, bias = prepare(
        first[None], q, qt, g, gt, w_uk, w_uv, doc_start[None]
    )
    ds, keep, send = attend(
        info, qct, glt, bias, latent, mine, theirs, qc, gl, factor, chips
    )
    both = keep + swap_cores(send).astype(F32)
    total = both[BACK]
    for distance in range(BACK, 0, -1):
        total = total + move(both[BACK - distance].astype(BF16), -distance).astype(F32)
    dq = query_gradient(info, ds, ukt, latent, mine, theirs, factor)
    grad_query = jnp.transpose(dq, (1, 0, 2))
    grad_latent = lax.dynamic_index_in_dim(total, chip, 0, False)
    rounded = total.astype(BF16)
    for step in range(1, chips):
        piece = lax.dynamic_index_in_dim(rounded, (chip + step) % chips, 0, False)
        route = [(k, (k + step * CORES) % heads) for k in range(heads)]
        grad_latent = grad_latent + lax.ppermute(piece, "head", route).astype(F32)
    return grad_query, grad_latent


def solution(mesh):
    placed = (
        P("seq", "head", None),
        P("seq", "head", None),
        P("seq", None),
        P("head", None, None),
        P("head", None, None),
        P("seq"),
    )
    return jax.shard_map(
        shards,
        mesh=mesh,
        in_specs=placed,
        out_specs=(P("seq", "head", None), P(("seq", "head"), None)),
        check_vma=False,
    )
```

```python
import functools
import math

import jax
import jax.numpy as jnp
from jax import lax
from jax.experimental import pallas as pl
from jax.experimental.pallas import tpu as pltpu
from jax.sharding import PartitionSpec as P

BACK = 3
CORES = 2
BF16 = jnp.bfloat16
F32 = jnp.float32


def dot(a, b, contract=((1,), (0,))):
    return lax.dot_general(a, b, (contract, ((), ())), preferred_element_type=F32)


LOWEST = -1e30


def prepare_kernel(
    first_ref, qt_ref, gt_ref, uk_ref, uv_ref, start_ref,
    qct_ref, qc_ref, glt_ref, gl_ref, bias_ref,
):
    latw, nope = uk_ref.shape[1:]
    uk, uv = uk_ref[0], uv_ref[0]
    qct_ref[0, :latw] = dot(uk, qt_ref[0, :nope]).astype(BF16)
    qct_ref[0, latw:] = qt_ref[0, nope:]
    qc_ref[:, :latw] = dot(qt_ref[0, :nope].T, uk, ((1,), (1,))).astype(BF16)
    qc_ref[:, latw:] = qt_ref[0, nope:].T
    glt_ref[0] = dot(uv, gt_ref[0]).astype(BF16)
    gl_ref[...] = dot(gt_ref[0].T, uv, ((1,), (1,))).astype(BF16)
    shape = bias_ref.shape
    tokens = shape[1]
    row = pl.program_id(0) * shape[0] + lax.broadcasted_iota(jnp.int32, shape, 0)
    kpos = first_ref[0] + row
    qpos = first_ref[0] + BACK * tokens + lax.broadcasted_iota(jnp.int32, shape, 1)
    visible = (kpos >= start_ref[...]) & (kpos <= qpos)
    bias_ref[...] = jnp.where(visible, 0.0, -jnp.inf).astype(F32)


def prepare(first, qt, gt, w_uk, w_uv, doc_start):
    heads, qw, tokens = qt.shape
    latw, nope = w_uk.shape[1:]
    vdim = gt.shape[1]
    width = latw + qw - nope
    span = (BACK + 1) * tokens
    one = lambda *dims: pl.BlockSpec((1, *dims), lambda h, s: (h, 0, 0))
    rows = lambda n, d: pl.BlockSpec((n, d), lambda h, s: (h, 0))
    return pl.pallas_call(
        prepare_kernel,
        out_shape=(
            jax.ShapeDtypeStruct((heads, width, tokens), BF16),
            jax.ShapeDtypeStruct((heads * tokens, width), BF16),
            jax.ShapeDtypeStruct((heads, latw, tokens), BF16),
            jax.ShapeDtypeStruct((heads * tokens, latw), BF16),
            jax.ShapeDtypeStruct((span, tokens), F32),
        ),
        grid_spec=pltpu.PrefetchScalarGridSpec(
            num_scalar_prefetch=1,
            grid=(heads,),
            in_specs=[
                one(qw, tokens), one(vdim, tokens), one(latw, nope), one(latw, vdim),
                pl.BlockSpec((1, tokens), lambda h, s: (0, 0)),
            ],
            out_specs=[
                one(width, tokens), rows(tokens, width), one(latw, tokens),
                rows(tokens, latw), rows(span // heads, tokens),
            ],
        ),
        cost_estimate=pl.CostEstimate(
            flops=8 * heads * tokens * latw * nope, transcendentals=0,
            bytes_accessed=16 << 20,
        ),
        name="prepare",
    )(first, qt, gt, w_uk, w_uv, doc_start)


def main_kernel(
    info_ref, qct_ref, glt_ref, bias_ref, own_ref,
    m3_ref, m2_ref, m1_ref, t3_ref, t2_ref, t1_ref, qc_hbm, gl_hbm,
    ds_ref, keep_ref, send_ref,
    keys_s, expo_s, dprob_s, p_s, ds_s, qc_s, gl_s, sems, *, factor,
):
    step = pl.program_id(0)
    core, low = info_ref[0], info_ref[1]
    span, tokens = bias_ref.shape
    pair, latw = glt_ref.shape[:2]
    half = tokens // CORES
    chunk = 64
    scale = factor * math.log2(math.e)

    @pl.when(step == 0)
    def _():
        pltpu.make_async_copy(qc_hbm, qc_s, sems.at[0]).start()
        pltpu.make_async_copy(gl_hbm, gl_s, sems.at[1]).start()
        for block, (mine, theirs) in enumerate(
            ((m3_ref, t3_ref), (m2_ref, t2_ref), (m1_ref, t1_ref))
        ):
            keys_s[pl.ds(pl.multiple_of(block * tokens + core * half, half), half)] = mine[...].T
            keys_s[pl.ds(pl.multiple_of(block * tokens + (1 - core) * half, half), half)] = theirs[...].T
        keys_s[BACK * tokens :] = own_ref[...].T

    def fold(x, op):
        return op(x.reshape(-1, 8, tokens), axis=0)

    def heads_from(begin):
        chunks = range(begin, span, chunk)
        for n in range(pair):
            lane = pl.ds(pl.multiple_of((step * pair + n) * tokens, tokens), tokens)
            tops, totals = [], []
            for block in range(begin, span, tokens):
                scores = dot(keys_s[block : block + tokens], qct_ref[n]) * scale
                scores = scores + bias_ref[block : block + tokens]
                for c in range(0, tokens, chunk):
                    s = scores[c : c + chunk]
                    top = jnp.max(fold(s, jnp.max), axis=0, keepdims=True)
                    top = jnp.maximum(top, LOWEST)
                    e = jnp.exp2(s - top)
                    expo_s[n, block + c : block + c + chunk] = e
                    tops.append(top)
                    totals.append(jnp.sum(fold(e, jnp.sum), axis=0, keepdims=True))
            top = functools.reduce(jnp.maximum, tops)
            weights = [jnp.exp2(t - top) for t in tops]
            total = sum(w * t for w, t in zip(weights, totals))
            inverse = 1.0 / total
            delta = jnp.zeros((8, tokens), F32)
            for block in range(begin, span, tokens):
                dprob = dot(keys_s[block : block + tokens, :latw], glt_ref[n])
                for c in range(0, tokens, chunk):
                    at = slice(block + c, block + c + chunk)
                    weight = weights[(block + c - begin) // chunk] * inverse
                    p = (expo_s[n, at] * weight).astype(BF16)
                    dp = dprob[c : c + chunk]
                    p_s[at, lane] = p
                    dprob_s[n, at] = dp
                    delta = delta + fold(p.astype(F32) * dp, jnp.sum)
            delta = jnp.sum(delta, axis=0, keepdims=True)
            for c in chunks:
                at = slice(c, c + chunk)
                ds = (p_s[at, lane].astype(F32) * (dprob_s[n, at] - delta)).astype(BF16)
                ds_s[at, lane] = ds
                ds_ref[n, at] = ds
            if begin:
                zero = jnp.zeros((begin, tokens), BF16)
                ds_ref[n, :begin] = zero

    for block in range(BACK + 1):
        pl.when(low == block)(functools.partial(heads_from, block * tokens))

    @pl.when(step == pl.num_programs(0) - 1)
    def _():
        pltpu.make_async_copy(qc_hbm, qc_s, sems.at[0]).wait()
        pltpu.make_async_copy(gl_hbm, gl_s, sems.at[1]).wait()
        groups, piece = keep_ref.shape[1:3]

        def gradient(block, _):
            at = pl.ds(pl.multiple_of(block * tokens, tokens), tokens)

            def put(column, value):
                sides = value.reshape(groups, CORES, piece, -1)
                zeroth, first = sides[:, 0], sides[:, 1]
                keep_ref[block, :, :, column] = jnp.where(core == 0, zeroth, first)
                send_ref[block, :, :, column] = jnp.where(core == 0, first, zeroth).astype(BF16)

            key = dot(ds_s[at], qc_s[...]) * factor
            put(slice(0, latw), key[:, :latw] + dot(p_s[at], gl_s[...]))
            put(slice(latw, None), key[:, latw:])
            return 0

        def blank(block, _):
            keep_ref[block] = jnp.zeros(keep_ref.shape[1:], F32)
            send_ref[block] = jnp.zeros(send_ref.shape[1:], BF16)
            return 0

        lax.fori_loop(0, low, blank, 0)
        lax.fori_loop(low, BACK + 1, gradient, 0)


def attend(info, qct, glt, bias, own, mine, theirs, qc, gl, factor, groups, pair=2):
    heads, width, tokens = qct.shape
    latw = glt.shape[1]
    span = bias.shape[0]
    piece = tokens // CORES // groups
    head = lambda d: pl.BlockSpec((pair, d, tokens), lambda h, s: (h, 0, 0))
    whole = lambda a: pl.BlockSpec(a.shape, lambda h, s: (0,) * a.ndim)
    out = (BACK + 1, groups, piece, width)
    return pl.pallas_call(
        functools.partial(main_kernel, factor=factor),
        out_shape=(
            jax.ShapeDtypeStruct((heads, span, tokens), BF16),
            jax.ShapeDtypeStruct(out, F32),
            jax.ShapeDtypeStruct(out, BF16),
        ),
        grid_spec=pltpu.PrefetchScalarGridSpec(
            num_scalar_prefetch=1,
            grid=(heads // pair,),
            in_specs=[head(width), head(latw), whole(bias), whole(own)]
            + [whole(a) for a in (*mine, *theirs)]
            + [pl.BlockSpec(memory_space=pl.ANY)] * 2,
            out_specs=[
                pl.BlockSpec((pair, span, tokens), lambda h, s: (h, 0, 0)),
                pl.BlockSpec(out, lambda h, s: (0, 0, 0, 0)),
                pl.BlockSpec(out, lambda h, s: (0, 0, 0, 0)),
            ],
            scratch_shapes=[
                pltpu.VMEM((span, width), BF16),
                pltpu.VMEM((pair, span, tokens), F32),
                pltpu.VMEM((pair, span, tokens), F32),
                pltpu.VMEM((span, heads * tokens), BF16),
                pltpu.VMEM((span, heads * tokens), BF16),
                pltpu.VMEM(qc.shape, BF16),
                pltpu.VMEM(gl.shape, BF16),
                pltpu.SemaphoreType.DMA((2,)),
            ],
        ),
        compiler_params=pltpu.CompilerParams(vmem_limit_bytes=58 << 20),
        cost_estimate=pl.CostEstimate(
            flops=2 * heads * tokens * span * (2 * width + 2 * latw),
            transcendentals=heads * tokens * span, bytes_accessed=24 << 20,
        ),
        name="attend",
    )(info, qct, glt, bias, own, *mine, *theirs, qc, gl)


def query_kernel(
    info_ref, ds_ref, uk_ref, own_ref, m3_ref, m2_ref, m1_ref, t3_ref, t2_ref, t1_ref,
    out_ref, keys_s, *, factor,
):
    core = info_ref[0]
    width, tokens = own_ref.shape
    half = tokens // CORES
    latw, nope = uk_ref.shape[1:]

    @pl.when(pl.program_id(0) == 0)
    def _():
        for block, (mine, theirs) in enumerate(
            ((m3_ref, t3_ref), (m2_ref, t2_ref), (m1_ref, t1_ref))
        ):
            keys_s[:, pl.ds(pl.multiple_of(block * tokens + core * half, half), half)] = mine[...]
            keys_s[:, pl.ds(pl.multiple_of(block * tokens + (1 - core) * half, half), half)] = theirs[...]
        keys_s[:, BACK * tokens :] = own_ref[...]

    dq = dot(keys_s[...], ds_ref[0]) * factor
    dq_nope = dot(uk_ref[0], dq[:latw].astype(BF16), ((0,), (0,)))
    out_ref[0, :nope] = dq_nope.astype(BF16)
    out_ref[0, nope:] = dq[latw:].astype(BF16)


def query_gradient(info, ds, w_uk, own, mine, theirs, factor):
    heads, span, tokens = ds.shape
    latw, nope = w_uk.shape[1:]
    width = own.shape[0]
    qw = nope + width - latw
    whole = lambda a: pl.BlockSpec(a.shape, lambda h, s: (0,) * a.ndim)
    return pl.pallas_call(
        functools.partial(query_kernel, factor=factor),
        out_shape=jax.ShapeDtypeStruct((heads, qw, tokens), BF16),
        grid_spec=pltpu.PrefetchScalarGridSpec(
            num_scalar_prefetch=1,
            grid=(heads,),
            in_specs=[
                pl.BlockSpec((1, span, tokens), lambda h, s: (h, 0, 0)),
                pl.BlockSpec((1, latw, nope), lambda h, s: (h, 0, 0)),
                whole(own),
            ]
            + [whole(a) for a in (*mine, *theirs)],
            out_specs=pl.BlockSpec((1, qw, tokens), lambda h, s: (h, 0, 0)),
            scratch_shapes=[pltpu.VMEM((width, span), BF16)],
        ),
        compiler_params=pltpu.CompilerParams(vmem_limit_bytes=32 << 20),
        cost_estimate=pl.CostEstimate(
            flops=2 * heads * tokens * (span * width + latw * nope),
            transcendentals=0, bytes_accessed=8 << 20,
        ),
        name="query_gradient",
    )(info, ds, w_uk, own, *mine, *theirs)


def along_seq(distance, crossings=True):
    devices = lax.axis_size("seq")
    pairs = []
    for source in range(devices):
        target = source + distance
        if 0 <= target < devices:
            crossing = (2 * source < devices) != (2 * target < devices)
            if crossings or not crossing:
                pairs += between(source, target, crossing)
    return pairs


def between(source, target, mirrored=False):
    heads = lax.axis_size("head")
    pairs = []
    for head in range(heads):
        chip, core = divmod(head, CORES)
        if mirrored:
            chip = heads // CORES - 1 - chip
        pairs.append((source * heads + head, target * heads + chip * CORES + core))
    return pairs


def send(value, pairs):
    return lax.ppermute(value, ("seq", "head"), pairs)


def swap_cores(value):
    return lax.ppermute(value, "head", [(k, k ^ 1) for k in range(lax.axis_size("head"))])


def shards(queries, grad_out, latent, w_uk, w_uv, doc_start):
    tokens, width = latent.shape
    factor = queries.shape[2] ** (-0.5)
    seq, head = lax.axis_index("seq"), lax.axis_index("head")
    heads = lax.axis_size("head")
    chips = heads // CORES
    core, chip = head % CORES, head // CORES
    half = tokens // CORES

    own = latent.T
    part = lax.dynamic_slice_in_dim(own, core * half, half, 1)
    far = send(part, along_seq(3))
    near = [send(part, along_seq(distance, False)) for distance in (2, 1)]

    first = (seq - BACK) * tokens
    low = jnp.maximum(doc_start[0] - first, 0) // tokens
    info = jnp.stack([core, low]).astype(jnp.int32)
    qt = jnp.transpose(queries, (1, 2, 0))
    gt = jnp.transpose(grad_out, (1, 2, 0))
    prepared = prepare(first[None], qt, gt, w_uk, w_uv, doc_start[None])
    far, prepared = lax.optimization_barrier((far, prepared))
    qct, qc, glt, gl, bias = prepared

    middle = lax.axis_size("seq") // 2
    relays = (
        between(middle + 1, middle) + between(middle + 2, middle + 1),
        between(middle + 2, middle),
    )
    mine = [far] + [direct + send(far, relay) for direct, relay in zip(near, relays)]
    theirs = [swap_cores(piece) for piece in mine]

    ds, keep, away = attend(
        info, qct, glt, bias, own, mine, theirs, qc, gl, factor, chips
    )
    both = keep + swap_cores(away).astype(F32)
    total = both[BACK]
    back = [
        send(both[BACK - distance].astype(BF16), along_seq(-distance))
        for distance in range(BACK, 0, -1)
    ]
    dq = query_gradient(info, ds, w_uk, own, mine, theirs, factor)
    back, dq = lax.optimization_barrier((back, dq))
    for piece in back:
        total = total + piece.astype(F32)
    grad_query = jnp.transpose(dq, (2, 0, 1))
    grad_latent = lax.dynamic_index_in_dim(total, chip, 0, False)
    rounded = total.astype(BF16)
    for step in range(1, chips):
        piece = lax.dynamic_index_in_dim(rounded, (chip + step) % chips, 0, False)
        route = [(k, (k + step * CORES) % heads) for k in range(heads)]
        grad_latent = grad_latent + lax.ppermute(piece, "head", route).astype(F32)
    return grad_query, grad_latent


def solution(mesh):
    placed = (
        P("seq", "head", None),
        P("seq", "head", None),
        P("seq", None),
        P("head", None, None),
        P("head", None, None),
        P("seq"),
    )
    return jax.shard_map(
        shards,
        mesh=mesh,
        in_specs=placed,
        out_specs=(P("seq", "head", None), P(("seq", "head"), None)),
        check_vma=False,
    )
```

```python
import functools
import math

import jax
import jax.numpy as jnp
from jax import lax
from jax.experimental import pallas as pl
from jax.experimental.pallas import tpu as pltpu
from jax.sharding import PartitionSpec as P

BACK = 3
CORES = 2
BF16 = jnp.bfloat16
F32 = jnp.float32


def dot(a, b, contract=((1,), (0,))):
    return lax.dot_general(a, b, (contract, ((), ())), preferred_element_type=F32)


LOWEST = -1e30


def prepare_kernel(
    info_ref, qt_ref, gt_ref, uk_ref, uv_ref, start_ref,
    qct_ref, qc_ref, glt_ref, gl_ref, bias_ref,
):
    pair, latw, nope = uk_ref.shape
    tokens = qt_ref.shape[2]
    for n in range(pair):
        uk, uv = uk_ref[n], uv_ref[n]
        rows = slice(n * tokens, (n + 1) * tokens)
        qct_ref[n, :latw] = dot(uk, qt_ref[n, :nope]).astype(BF16)
        qct_ref[n, latw:] = qt_ref[n, nope:]
        qc_ref[rows, :latw] = dot(qt_ref[n, :nope].T, uk, ((1,), (1,))).astype(BF16)
        qc_ref[rows, latw:] = qt_ref[n, nope:].T
        glt_ref[n] = dot(uv, gt_ref[n]).astype(BF16)
        gl_ref[rows] = dot(gt_ref[n].T, uv, ((1,), (1,))).astype(BF16)
    shape = bias_ref.shape
    row = pl.program_id(0) * shape[0] + lax.broadcasted_iota(jnp.int32, shape, 0)
    kpos = info_ref[1] + row
    qpos = info_ref[1] + BACK * tokens + lax.broadcasted_iota(jnp.int32, shape, 1)
    visible = (kpos >= start_ref[...]) & (kpos <= qpos)
    bias_ref[...] = jnp.where(visible, 0.0, -jnp.inf).astype(F32)


def prepare(info, qt, gt, w_uk, w_uv, doc_start, pair=2):
    heads, qw, tokens = qt.shape
    latw, nope = w_uk.shape[1:]
    vdim = gt.shape[1]
    width = latw + qw - nope
    span = (BACK + 1) * tokens
    one = lambda *dims: pl.BlockSpec((pair, *dims), lambda h, s: (h, 0, 0))
    rows = lambda n, d: pl.BlockSpec((pair * n, d), lambda h, s: (h, 0))
    return pl.pallas_call(
        prepare_kernel,
        out_shape=(
            jax.ShapeDtypeStruct((heads, width, tokens), BF16),
            jax.ShapeDtypeStruct((heads * tokens, width), BF16),
            jax.ShapeDtypeStruct((heads, latw, tokens), BF16),
            jax.ShapeDtypeStruct((heads * tokens, latw), BF16),
            jax.ShapeDtypeStruct((span, tokens), F32),
        ),
        grid_spec=pltpu.PrefetchScalarGridSpec(
            num_scalar_prefetch=1,
            grid=(heads // pair,),
            in_specs=[
                one(qw, tokens), one(vdim, tokens), one(latw, nope), one(latw, vdim),
                pl.BlockSpec((1, tokens), lambda h, s: (0, 0)),
            ],
            out_specs=[
                one(width, tokens), rows(tokens, width), one(latw, tokens),
                rows(tokens, latw), rows(span // heads, tokens),
            ],
        ),
        compiler_params=pltpu.CompilerParams(vmem_limit_bytes=16 << 20),
        cost_estimate=pl.CostEstimate(
            flops=8 * heads * tokens * latw * nope, transcendentals=0,
            bytes_accessed=16 << 20,
        ),
        name="prepare",
    )(info, qt, gt, w_uk, w_uv, doc_start)


def main_kernel(
    info_ref, start_ref, qct_ref, glt_ref, bias_ref, own_ref,
    m3_ref, m2_ref, m1_ref, t3_ref, t2_ref, t1_ref, qc_hbm, gl_hbm,
    ds_ref, keep_ref, send_ref,
    keys_s, expo_s, dprob_s, p_s, ds_s, qc_s, gl_s, sems, *, factor,
):
    step = pl.program_id(0)
    core = info_ref[0]
    span, tokens = bias_ref.shape
    low = jnp.maximum(start_ref[0] - info_ref[1], 0) // tokens
    pair, latw = glt_ref.shape[:2]
    half = tokens // CORES
    chunk = 64
    scale = factor * math.log2(math.e)

    @pl.when(step == 0)
    def _():
        pltpu.make_async_copy(qc_hbm, qc_s, sems.at[0]).start()
        pltpu.make_async_copy(gl_hbm, gl_s, sems.at[1]).start()
        for block, (mine, theirs) in enumerate(
            ((m3_ref, t3_ref), (m2_ref, t2_ref), (m1_ref, t1_ref))
        ):
            keys_s[pl.ds(pl.multiple_of(block * tokens + core * half, half), half)] = mine[...].T
            keys_s[pl.ds(pl.multiple_of(block * tokens + (1 - core) * half, half), half)] = theirs[...].T
        keys_s[BACK * tokens :] = own_ref[...].T

    def fold(x, op):
        return op(x.reshape(-1, 8, tokens), axis=0)

    def heads_from(begin):
        chunks = range(begin, span, chunk)
        for n in range(pair):
            lane = pl.ds(pl.multiple_of((step * pair + n) * tokens, tokens), tokens)
            tops, totals = [], []
            for block in range(begin, span, tokens):
                scores = dot(keys_s[block : block + tokens], qct_ref[n]) * scale
                scores = scores + bias_ref[block : block + tokens]
                for c in range(0, tokens, chunk):
                    s = scores[c : c + chunk]
                    top = jnp.max(fold(s, jnp.max), axis=0, keepdims=True)
                    top = jnp.maximum(top, LOWEST)
                    e = jnp.exp2(s - top)
                    expo_s[n, block + c : block + c + chunk] = e
                    tops.append(top)
                    totals.append(jnp.sum(fold(e, jnp.sum), axis=0, keepdims=True))
            top = functools.reduce(jnp.maximum, tops)
            weights = [jnp.exp2(t - top) for t in tops]
            total = sum(w * t for w, t in zip(weights, totals))
            inverse = 1.0 / total
            delta = jnp.zeros((8, tokens), F32)
            for block in range(begin, span, tokens):
                dprob = dot(keys_s[block : block + tokens, :latw], glt_ref[n])
                for c in range(0, tokens, chunk):
                    at = slice(block + c, block + c + chunk)
                    weight = weights[(block + c - begin) // chunk] * inverse
                    p = (expo_s[n, at] * weight).astype(BF16)
                    dp = dprob[c : c + chunk]
                    p_s[at, lane] = p
                    dprob_s[n, at] = dp
                    delta = delta + fold(p.astype(F32) * dp, jnp.sum)
            delta = jnp.sum(delta, axis=0, keepdims=True)
            for c in chunks:
                at = slice(c, c + chunk)
                ds = (p_s[at, lane].astype(F32) * (dprob_s[n, at] - delta)).astype(BF16)
                ds_s[at, lane] = ds
                ds_ref[n, at] = ds
            if begin:
                zero = jnp.zeros((begin, tokens), BF16)
                ds_ref[n, :begin] = zero

    for block in range(BACK + 1):
        pl.when(low == block)(functools.partial(heads_from, block * tokens))

    @pl.when(step == pl.num_programs(0) - 1)
    def _():
        pltpu.make_async_copy(qc_hbm, qc_s, sems.at[0]).wait()
        pltpu.make_async_copy(gl_hbm, gl_s, sems.at[1]).wait()
        groups, piece = keep_ref.shape[1:3]

        def gradient(block, _):
            at = pl.ds(pl.multiple_of(block * tokens, tokens), tokens)

            def put(column, value):
                sides = value.reshape(groups, CORES, piece, -1)
                zeroth, first = sides[:, 0], sides[:, 1]
                keep_ref[block, :, :, column] = jnp.where(core == 0, zeroth, first).astype(BF16)
                send_ref[block, :, :, column] = jnp.where(core == 0, first, zeroth).astype(BF16)

            key = dot(ds_s[at], qc_s[...]) * factor
            put(slice(0, latw), key[:, :latw] + dot(p_s[at], gl_s[...]))
            put(slice(latw, None), key[:, latw:])
            return 0

        def blank(block, _):
            keep_ref[block] = jnp.zeros(keep_ref.shape[1:], BF16)
            send_ref[block] = jnp.zeros(send_ref.shape[1:], BF16)
            return 0

        lax.fori_loop(0, low, blank, 0)
        lax.fori_loop(low, BACK + 1, gradient, 0)


def attend(info, doc_start, qct, glt, bias, own, mine, theirs, qc, gl, factor, groups, pair=2):
    heads, width, tokens = qct.shape
    latw = glt.shape[1]
    span = bias.shape[0]
    piece = tokens // CORES // groups
    head = lambda d: pl.BlockSpec((pair, d, tokens), lambda h, *_: (h, 0, 0))
    whole = lambda a: pl.BlockSpec(a.shape, lambda h, *_: (0,) * a.ndim)
    out = (BACK + 1, groups, piece, width)
    return pl.pallas_call(
        functools.partial(main_kernel, factor=factor),
        out_shape=(
            pltpu.HBM((heads, span, tokens), BF16),
            jax.ShapeDtypeStruct(out, BF16),
            jax.ShapeDtypeStruct(out, BF16),
        ),
        grid_spec=pltpu.PrefetchScalarGridSpec(
            num_scalar_prefetch=2,
            grid=(heads // pair,),
            in_specs=[head(width), head(latw), whole(bias), whole(own)]
            + [whole(a) for a in (*mine, *theirs)]
            + [pl.BlockSpec(memory_space=pl.ANY)] * 2,
            out_specs=[
                head(span),
                pl.BlockSpec(out, lambda h, *_: (0, 0, 0, 0)),
                pl.BlockSpec(out, lambda h, *_: (0, 0, 0, 0)),
            ],
            scratch_shapes=[
                pltpu.VMEM((span, width), BF16),
                pltpu.VMEM((pair, span, tokens), F32),
                pltpu.VMEM((pair, span, tokens), F32),
                pltpu.VMEM((span, heads * tokens), BF16),
                pltpu.VMEM((span, heads * tokens), BF16),
                pltpu.VMEM(qc.shape, BF16),
                pltpu.VMEM(gl.shape, BF16),
                pltpu.SemaphoreType.DMA((2,)),
            ],
        ),
        compiler_params=pltpu.CompilerParams(vmem_limit_bytes=36 << 20),
        cost_estimate=pl.CostEstimate(
            flops=2 * heads * tokens * span * (2 * width + 2 * latw),
            transcendentals=heads * tokens * span, bytes_accessed=24 << 20,
        ),
        name="attend",
    )(info, doc_start, qct, glt, bias, own, *mine, *theirs, qc, gl)


def query_kernel(
    info_ref, ds_ref, uk_ref, own_ref, m3_ref, m2_ref, m1_ref, t3_ref, t2_ref, t1_ref,
    out_ref, keys_s, *, factor,
):
    core = info_ref[0]
    width, tokens = own_ref.shape
    half = tokens // CORES
    latw, nope = uk_ref.shape[1:]

    @pl.when(pl.program_id(0) == 0)
    def _():
        for block, (mine, theirs) in enumerate(
            ((m3_ref, t3_ref), (m2_ref, t2_ref), (m1_ref, t1_ref))
        ):
            keys_s[:, pl.ds(pl.multiple_of(block * tokens + core * half, half), half)] = mine[...]
            keys_s[:, pl.ds(pl.multiple_of(block * tokens + (1 - core) * half, half), half)] = theirs[...]
        keys_s[:, BACK * tokens :] = own_ref[...]

    dq = dot(keys_s[...], ds_ref[0]) * factor
    dq_nope = dot(uk_ref[0], dq[:latw].astype(BF16), ((0,), (0,)))
    out_ref[0, :nope] = dq_nope.astype(BF16)
    out_ref[0, nope:] = dq[latw:].astype(BF16)


def query_gradient(info, ds, w_uk, own, mine, theirs, factor):
    heads, span, tokens = ds.shape
    latw, nope = w_uk.shape[1:]
    width = own.shape[0]
    qw = nope + width - latw
    whole = lambda a: pl.BlockSpec(a.shape, lambda h, s: (0,) * a.ndim)
    return pl.pallas_call(
        functools.partial(query_kernel, factor=factor),
        out_shape=jax.ShapeDtypeStruct((heads, qw, tokens), BF16),
        grid_spec=pltpu.PrefetchScalarGridSpec(
            num_scalar_prefetch=1,
            grid=(heads,),
            in_specs=[
                pl.BlockSpec((1, span, tokens), lambda h, s: (h, 0, 0)),
                pl.BlockSpec((1, latw, nope), lambda h, s: (h, 0, 0)),
                whole(own),
            ]
            + [whole(a) for a in (*mine, *theirs)],
            out_specs=pl.BlockSpec((1, qw, tokens), lambda h, s: (h, 0, 0)),
            scratch_shapes=[pltpu.VMEM((width, span), BF16)],
        ),
        compiler_params=pltpu.CompilerParams(vmem_limit_bytes=16 << 20),
        cost_estimate=pl.CostEstimate(
            flops=2 * heads * tokens * (span * width + latw * nope),
            transcendentals=0, bytes_accessed=8 << 20,
        ),
        name="query_gradient",
    )(info, ds, w_uk, own, *mine, *theirs)


def along_seq(distance, crossings=True):
    devices = lax.axis_size("seq")
    pairs = []
    for source in range(devices):
        target = source + distance
        if 0 <= target < devices:
            crossing = (2 * source < devices) != (2 * target < devices)
            if crossings or not crossing:
                pairs += between(source, target, crossing)
    return pairs


def between(source, target, mirrored=False):
    heads = lax.axis_size("head")
    pairs = []
    for head in range(heads):
        chip, core = divmod(head, CORES)
        if mirrored:
            chip = heads // CORES - 1 - chip
        pairs.append((source * heads + head, target * heads + chip * CORES + core))
    return pairs


def send(value, pairs):
    return lax.ppermute(value, ("seq", "head"), pairs)


def in_hbm(value):
    return pltpu.with_memory_space_constraint(value, pltpu.HBM)


def swap_cores(value):
    return lax.ppermute(value, "head", [(k, k ^ 1) for k in range(lax.axis_size("head"))])


def shards(queries, grad_out, latent, w_uk, w_uv, doc_start):
    tokens, width = latent.shape
    factor = queries.shape[2] ** (-0.5)
    seq, head = lax.axis_index("seq"), lax.axis_index("head")
    heads = lax.axis_size("head")
    chips = heads // CORES
    core, chip = head % CORES, head // CORES
    half = tokens // CORES

    own = latent.T
    part = lax.dynamic_slice_in_dim(own, core * half, half, 1)
    near = [send(part, along_seq(distance, False)) for distance in (2, 1)]
    far = send(part, along_seq(3))

    info = jnp.stack([core, (seq - BACK) * tokens]).astype(jnp.int32)
    qt = jnp.transpose(queries, (1, 2, 0))
    gt = jnp.transpose(grad_out, (1, 2, 0))
    prepared = prepare(info, in_hbm(qt), gt, in_hbm(w_uk), in_hbm(w_uv), doc_start[None])
    far, near, prepared = lax.optimization_barrier((far, near, prepared))
    qct, qc, glt, gl, bias = prepared

    middle = lax.axis_size("seq") // 2
    after, next_one, next_two = middle, middle + 1, middle + 2
    relays = (between(next_one, after) + between(next_two, next_one), between(next_two, after))
    returns = (between(after, next_one) + between(next_one, next_two), between(after, next_two))
    mine = [far] + [direct + send(far, relay) for direct, relay in zip(near, relays)]
    theirs = [swap_cores(piece) for piece in mine]

    ds, keep, away = attend(
        info, doc_start, qct, glt, bias, own, mine, theirs, qc, gl, factor, chips
    )
    arrived = swap_cores(away)
    far, *near, total = list(keep + arrived)
    for piece, route in zip(near, returns):
        far = far + send(piece, route)
    back = [send(piece, along_seq(-distance, False)) for piece, distance in zip(near, (2, 1))]
    back.append(send(far, along_seq(-3)))
    dq = query_gradient(info, in_hbm(ds), in_hbm(w_uk), own, mine, theirs, factor)
    back, dq = lax.optimization_barrier((back, dq))
    total = total.astype(F32)
    for piece in back:
        total = total + piece.astype(F32)
    grad_query = jnp.transpose(dq, (2, 0, 1))
    grad_latent = lax.dynamic_index_in_dim(total, chip, 0, False)
    rounded = total.astype(BF16)
    for step in range(1, chips):
        piece = lax.dynamic_index_in_dim(rounded, (chip + step) % chips, 0, False)
        route = [(k, (k + step * CORES) % heads) for k in range(heads)]
        grad_latent = grad_latent + lax.ppermute(piece, "head", route).astype(F32)
    return grad_query, grad_latent


def solution(mesh):
    placed = (
        P("seq", "head", None),
        P("seq", "head", None),
        P("seq", None),
        P("head", None, None),
        P("head", None, None),
        P("seq"),
    )
    return jax.shard_map(
        shards,
        mesh=mesh,
        in_specs=placed,
        out_specs=(P("seq", "head", None), P(("seq", "head"), None)),
        check_vma=False,
    )
```

```python
import functools
import math

import jax
import jax.numpy as jnp
from jax import lax
from jax.experimental import pallas as pl
from jax.experimental.pallas import tpu as pltpu
from jax.sharding import PartitionSpec as P

BACK = 3
CORES = 2
BF16 = jnp.bfloat16
F32 = jnp.float32


def dot(a, b, contract=((1,), (0,))):
    return lax.dot_general(a, b, (contract, ((), ())), preferred_element_type=F32)


LOWEST = -1e30


def prepare_kernel(
    info_ref, qt_ref, gt_ref, uk_ref, uv_ref, start_ref,
    qct_ref, qc_ref, glt_ref, gl_ref, bias_ref,
):
    pair, latw, nope = uk_ref.shape
    tokens = qt_ref.shape[2]
    for n in range(pair):
        uk, uv = uk_ref[n], uv_ref[n]
        rows = slice(n * tokens, (n + 1) * tokens)
        qct_ref[n, :latw] = dot(uk, qt_ref[n, :nope]).astype(BF16)
        qct_ref[n, latw:] = qt_ref[n, nope:]
        qc_ref[rows, :latw] = dot(qt_ref[n, :nope].T, uk, ((1,), (1,))).astype(BF16)
        qc_ref[rows, latw:] = qt_ref[n, nope:].T
        glt_ref[n] = dot(uv, gt_ref[n]).astype(BF16)
        gl_ref[rows] = dot(gt_ref[n].T, uv, ((1,), (1,))).astype(BF16)
    shape = bias_ref.shape
    row = pl.program_id(0) * shape[0] + lax.broadcasted_iota(jnp.int32, shape, 0)
    kpos = info_ref[1] + row
    qpos = info_ref[1] + BACK * tokens + lax.broadcasted_iota(jnp.int32, shape, 1)
    visible = (kpos >= start_ref[...]) & (kpos <= qpos)
    bias_ref[...] = jnp.where(visible, 0.0, -jnp.inf).astype(F32)


def prepare(info, qt, gt, w_uk, w_uv, doc_start, pair=2):
    heads, qw, tokens = qt.shape
    latw, nope = w_uk.shape[1:]
    vdim = gt.shape[1]
    width = latw + qw - nope
    span = (BACK + 1) * tokens
    one = lambda *dims: pl.BlockSpec((pair, *dims), lambda h, s: (h, 0, 0))
    rows = lambda n, d: pl.BlockSpec((pair * n, d), lambda h, s: (h, 0))
    return pl.pallas_call(
        prepare_kernel,
        out_shape=(
            jax.ShapeDtypeStruct((heads, width, tokens), BF16),
            jax.ShapeDtypeStruct((heads * tokens, width), BF16),
            jax.ShapeDtypeStruct((heads, latw, tokens), BF16),
            jax.ShapeDtypeStruct((heads * tokens, latw), BF16),
            jax.ShapeDtypeStruct((span, tokens), F32),
        ),
        grid_spec=pltpu.PrefetchScalarGridSpec(
            num_scalar_prefetch=1,
            grid=(heads // pair,),
            in_specs=[
                one(qw, tokens), one(vdim, tokens), one(latw, nope), one(latw, vdim),
                pl.BlockSpec((1, tokens), lambda h, s: (0, 0)),
            ],
            out_specs=[
                one(width, tokens), rows(tokens, width), one(latw, tokens),
                rows(tokens, latw), rows(span // heads, tokens),
            ],
        ),
        compiler_params=pltpu.CompilerParams(vmem_limit_bytes=16 << 20),
        cost_estimate=pl.CostEstimate(
            flops=8 * heads * tokens * latw * nope, transcendentals=0,
            bytes_accessed=16 << 20,
        ),
        name="prepare",
    )(info, qt, gt, w_uk, w_uv, doc_start)


def join(block_ref, core, mine_ref, theirs_ref):
    rows = mine_ref.shape[0]
    block_ref[pl.ds(pl.multiple_of(core * rows, rows), rows)] = mine_ref[...]
    block_ref[pl.ds(pl.multiple_of((1 - core) * rows, rows), rows)] = theirs_ref[...]


def main_kernel(
    info_ref, start_ref, qct_ref, glt_ref, bias_ref, own_ref,
    m3_ref, m2_ref, m1_ref, t3_ref, t2_ref, t1_ref, qc_hbm, gl_hbm,
    ds_ref, keep_ref, send_ref,
    block_s, keys_s, expo_s, dprob_s, p_s, ds_s, qc_s, gl_s, sems, *, factor,
):
    step = pl.program_id(0)
    core = info_ref[0]
    span, tokens = bias_ref.shape
    low = jnp.maximum(start_ref[0] - info_ref[1], 0) // tokens
    pair, latw = glt_ref.shape[:2]
    chunk = 64
    scale = factor * math.log2(math.e)

    @pl.when(step == 0)
    def _():
        pltpu.make_async_copy(qc_hbm, qc_s, sems.at[0]).start()
        pltpu.make_async_copy(gl_hbm, gl_s, sems.at[1]).start()
        for block, (mine, theirs) in enumerate(
            ((m3_ref, t3_ref), (m2_ref, t2_ref), (m1_ref, t1_ref))
        ):
            join(block_s.at[block % 2], core, mine, theirs)
            keys_s[block * tokens : (block + 1) * tokens] = block_s[block % 2].T
        keys_s[BACK * tokens :] = own_ref[...].T

    def fold(x, op):
        return op(x.reshape(-1, 8, tokens), axis=0)

    def heads_from(begin):
        chunks = range(begin, span, chunk)
        for n in range(pair):
            lane = pl.ds(pl.multiple_of((step * pair + n) * tokens, tokens), tokens)
            tops, totals = [], []
            for block in range(begin, span, tokens):
                scores = dot(keys_s[block : block + tokens], qct_ref[n]) * scale
                scores = scores + bias_ref[block : block + tokens]
                for c in range(0, tokens, chunk):
                    s = scores[c : c + chunk]
                    top = jnp.max(fold(s, jnp.max), axis=0, keepdims=True)
                    top = jnp.maximum(top, LOWEST)
                    e = jnp.exp2(s - top)
                    expo_s[n, block + c : block + c + chunk] = e
                    tops.append(top)
                    totals.append(jnp.sum(fold(e, jnp.sum), axis=0, keepdims=True))
            top = functools.reduce(jnp.maximum, tops)
            weights = [jnp.exp2(t - top) for t in tops]
            total = sum(w * t for w, t in zip(weights, totals))
            inverse = 1.0 / total
            delta = jnp.zeros((8, tokens), F32)
            for block in range(begin, span, tokens):
                dprob = dot(keys_s[block : block + tokens, :latw], glt_ref[n])
                for c in range(0, tokens, chunk):
                    at = slice(block + c, block + c + chunk)
                    weight = weights[(block + c - begin) // chunk] * inverse
                    p = (expo_s[n, at] * weight).astype(BF16)
                    dp = dprob[c : c + chunk]
                    p_s[at, lane] = p
                    dprob_s[n, at] = dp
                    delta = delta + fold(p.astype(F32) * dp, jnp.sum)
            delta = jnp.sum(delta, axis=0, keepdims=True)
            for c in chunks:
                at = slice(c, c + chunk)
                ds = (p_s[at, lane].astype(F32) * (dprob_s[n, at] - delta)).astype(BF16)
                ds_s[at, lane] = ds
                ds_ref[n, at] = ds
            if begin:
                zero = jnp.zeros((begin, tokens), BF16)
                ds_ref[n, :begin] = zero

    for block in range(BACK + 1):
        pl.when(low == block)(functools.partial(heads_from, block * tokens))

    @pl.when(step == pl.num_programs(0) - 1)
    def _():
        pltpu.make_async_copy(qc_hbm, qc_s, sems.at[0]).wait()
        pltpu.make_async_copy(gl_hbm, gl_s, sems.at[1]).wait()
        groups, piece = keep_ref.shape[1:3]

        def gradient(block, _):
            at = pl.ds(pl.multiple_of(block * tokens, tokens), tokens)

            def put(column, value):
                sides = value.reshape(groups, CORES, piece, -1)
                zeroth, first = sides[:, 0], sides[:, 1]
                keep_ref[block, :, :, column] = jnp.where(core == 0, zeroth, first).astype(BF16)
                send_ref[block, :, :, column] = jnp.where(core == 0, first, zeroth).astype(BF16)

            key = dot(ds_s[at], qc_s[...]) * factor
            put(slice(0, latw), key[:, :latw] + dot(p_s[at], gl_s[...]))
            put(slice(latw, None), key[:, latw:])
            return 0

        def blank(block, _):
            keep_ref[block] = jnp.zeros(keep_ref.shape[1:], BF16)
            send_ref[block] = jnp.zeros(send_ref.shape[1:], BF16)
            return 0

        lax.fori_loop(0, low, blank, 0)
        lax.fori_loop(low, BACK + 1, gradient, 0)


def attend(info, doc_start, qct, glt, bias, own, mine, theirs, qc, gl, factor, groups, pair=2):
    heads, width, tokens = qct.shape
    latw = glt.shape[1]
    span = bias.shape[0]
    piece = tokens // CORES // groups
    head = lambda d: pl.BlockSpec((pair, d, tokens), lambda h, *_: (h, 0, 0))
    whole = lambda a: pl.BlockSpec(a.shape, lambda h, *_: (0,) * a.ndim)
    out = (BACK + 1, groups, piece, width)
    return pl.pallas_call(
        functools.partial(main_kernel, factor=factor),
        out_shape=(
            pltpu.HBM((heads, span, tokens), BF16),
            jax.ShapeDtypeStruct(out, BF16),
            jax.ShapeDtypeStruct(out, BF16),
        ),
        grid_spec=pltpu.PrefetchScalarGridSpec(
            num_scalar_prefetch=2,
            grid=(heads // pair,),
            in_specs=[head(width), head(latw), whole(bias), whole(own)]
            + [whole(a) for a in (*mine, *theirs)]
            + [pl.BlockSpec(memory_space=pl.ANY)] * 2,
            out_specs=[
                head(span),
                pl.BlockSpec(out, lambda h, *_: (0, 0, 0, 0)),
                pl.BlockSpec(out, lambda h, *_: (0, 0, 0, 0)),
            ],
            scratch_shapes=[
                pltpu.VMEM((2, width, tokens), BF16),
                pltpu.VMEM((span, width), BF16),
                pltpu.VMEM((pair, span, tokens), F32),
                pltpu.VMEM((pair, span, tokens), F32),
                pltpu.VMEM((span, heads * tokens), BF16),
                pltpu.VMEM((span, heads * tokens), BF16),
                pltpu.VMEM(qc.shape, BF16),
                pltpu.VMEM(gl.shape, BF16),
                pltpu.SemaphoreType.DMA((2,)),
            ],
        ),
        compiler_params=pltpu.CompilerParams(vmem_limit_bytes=36 << 20),
        cost_estimate=pl.CostEstimate(
            flops=2 * heads * tokens * span * (2 * width + 2 * latw),
            transcendentals=heads * tokens * span, bytes_accessed=24 << 20,
        ),
        name="attend",
    )(info, doc_start, qct, glt, bias, own, *mine, *theirs, qc, gl)


def query_kernel(
    info_ref, ds_ref, uk_ref, own_ref, m3_ref, m2_ref, m1_ref, t3_ref, t2_ref, t1_ref,
    out_ref, keys_s, *, factor,
):
    core = info_ref[0]
    tokens = own_ref.shape[1]
    pair, latw, nope = uk_ref.shape

    @pl.when(pl.program_id(0) == 0)
    def _():
        for block, (mine, theirs) in enumerate(
            ((m3_ref, t3_ref), (m2_ref, t2_ref), (m1_ref, t1_ref))
        ):
            join(keys_s.at[:, pl.ds(block * tokens, tokens)], core, mine, theirs)
        keys_s[:, BACK * tokens :] = own_ref[...]

    for n in range(pair):
        dq = dot(keys_s[...], ds_ref[n]) * factor
        dq_nope = dot(uk_ref[n], dq[:latw].astype(BF16), ((0,), (0,)))
        out_ref[n, :nope] = dq_nope.astype(BF16)
        out_ref[n, nope:] = dq[latw:].astype(BF16)


def query_gradient(info, ds, w_uk, own, mine, theirs, factor, pair=2):
    heads, span, tokens = ds.shape
    latw, nope = w_uk.shape[1:]
    width = own.shape[0]
    qw = nope + width - latw
    whole = lambda a: pl.BlockSpec(a.shape, lambda h, s: (0,) * a.ndim)
    return pl.pallas_call(
        functools.partial(query_kernel, factor=factor),
        out_shape=jax.ShapeDtypeStruct((heads, qw, tokens), BF16),
        grid_spec=pltpu.PrefetchScalarGridSpec(
            num_scalar_prefetch=1,
            grid=(heads // pair,),
            in_specs=[
                pl.BlockSpec((pair, span, tokens), lambda h, s: (h, 0, 0)),
                pl.BlockSpec((pair, latw, nope), lambda h, s: (h, 0, 0)),
                whole(own),
            ]
            + [whole(a) for a in (*mine, *theirs)],
            out_specs=pl.BlockSpec((pair, qw, tokens), lambda h, s: (h, 0, 0)),
            scratch_shapes=[pltpu.VMEM((width, span), BF16)],
        ),
        compiler_params=pltpu.CompilerParams(vmem_limit_bytes=16 << 20),
        cost_estimate=pl.CostEstimate(
            flops=2 * heads * tokens * (span * width + latw * nope),
            transcendentals=0, bytes_accessed=8 << 20,
        ),
        name="query_gradient",
    )(info, ds, w_uk, own, *mine, *theirs)


def along_seq(distance, crossings=True):
    devices = lax.axis_size("seq")
    pairs = []
    for source in range(devices):
        target = source + distance
        if 0 <= target < devices:
            crossing = (2 * source < devices) != (2 * target < devices)
            if crossings or not crossing:
                pairs += between(source, target, crossing)
    return pairs


def between(source, target, mirrored=False):
    heads = lax.axis_size("head")
    pairs = []
    for head in range(heads):
        chip, core = divmod(head, CORES)
        if mirrored:
            chip = heads // CORES - 1 - chip
        pairs.append((source * heads + head, target * heads + chip * CORES + core))
    return pairs


def send(value, pairs):
    return lax.ppermute(value, ("seq", "head"), pairs)


def in_hbm(value):
    return pltpu.with_memory_space_constraint(value, pltpu.HBM)


def swap_cores(value):
    return lax.ppermute(value, "head", [(k, k ^ 1) for k in range(lax.axis_size("head"))])


def shards(queries, grad_out, latent, w_uk, w_uv, doc_start):
    tokens, width = latent.shape
    factor = queries.shape[2] ** (-0.5)
    seq, head = lax.axis_index("seq"), lax.axis_index("head")
    heads = lax.axis_size("head")
    chips = heads // CORES
    core, chip = head % CORES, head // CORES
    half = width // CORES

    own = latent.T
    part = lax.dynamic_slice_in_dim(own, core * half, half, 0)
    far = send(part, along_seq(3))
    near = [send(part, along_seq(distance, False)) for distance in (2, 1)]

    middle = lax.axis_size("seq") // 2
    after, next_one, next_two = middle, middle + 1, middle + 2
    relays = (between(next_one, after) + between(next_two, next_one), between(next_two, after))
    returns = (between(after, next_one) + between(next_one, next_two), between(after, next_two))

    info = jnp.stack([core, (seq - BACK) * tokens]).astype(jnp.int32)
    qt = jnp.transpose(queries, (1, 2, 0))
    gt = jnp.transpose(grad_out, (1, 2, 0))
    far, gt = lax.optimization_barrier((far, gt))
    relayed = [send(far, relay) for relay in relays]
    prepared = prepare(
        info, in_hbm(qt), gt, in_hbm(w_uk), in_hbm(w_uv), in_hbm(doc_start[None])
    )
    near, relayed, prepared = lax.optimization_barrier((near[::-1], relayed, prepared))
    qct, qc, glt, gl, bias = prepared
    mine = [far] + [direct + other for direct, other in zip(near[::-1], relayed)]
    theirs = [swap_cores(piece) for piece in mine]

    ds, keep, away = attend(
        info, doc_start, qct, glt, bias, own, mine, theirs, qc, gl, factor, chips
    )
    arrived = swap_cores(away)
    far, *near, total = list(keep + arrived)
    for piece, route in zip(near, returns):
        far = far + send(piece, route)
    far, near = lax.optimization_barrier((far, near))
    back = [send(piece, along_seq(-distance, False)) for piece, distance in zip(near, (2, 1))]
    back.append(send(far, along_seq(-3)))
    dq = query_gradient(info, in_hbm(ds), in_hbm(w_uk), own, mine, theirs, factor)
    back, dq = lax.optimization_barrier((back[::-1], dq))
    total = total.astype(F32)
    for piece in back:
        total = total + piece.astype(F32)
    grad_query = jnp.transpose(dq, (2, 0, 1))
    return grad_query, scatter_sum(total, chip)


def scatter_sum(total, chip):
    chips, rows, width = total.shape
    bit = 1
    while bit < chips:
        mine = chip // bit % 2
        halves = total.reshape(-1, 2, rows, width)
        away = lax.dynamic_index_in_dim(halves, 1 - mine, 1, False).astype(BF16)
        route = [(k, k ^ (bit * CORES)) for k in range(chips * CORES)]
        arrived = lax.ppermute(away, "head", route)
        total = lax.dynamic_index_in_dim(halves, mine, 1, False) + arrived.astype(F32)
        bit *= 2
    return total[0]


def solution(mesh):
    placed = (
        P("seq", "head", None),
        P("seq", "head", None),
        P("seq", None),
        P("head", None, None),
        P("head", None, None),
        P("seq"),
    )
    return jax.shard_map(
        shards,
        mesh=mesh,
        in_specs=placed,
        out_specs=(P("seq", "head", None), P(("seq", "head"), None)),
        check_vma=False,
    )
```

```python
import functools
import math

import jax
import jax.numpy as jnp
from jax import lax
from jax.experimental import pallas as pl
from jax.experimental.pallas import tpu as pltpu
from jax.sharding import PartitionSpec as P

BACK = 3
CORES = 2
BF16 = jnp.bfloat16
F32 = jnp.float32


def dot(a, b, contract=((1,), (0,))):
    return lax.dot_general(a, b, (contract, ((), ())), preferred_element_type=F32)


LOWEST = -1e30
CHUNK = 64
PAIR = 2


def prepare_kernel(
    info_ref, qt_ref, gt_ref, uk_ref, uv_ref, start_ref,
    qct_ref, qc_ref, glt_ref, gl_ref, bias_ref,
):
    pair, latw, nope = uk_ref.shape
    tokens = qt_ref.shape[2]
    for n in range(pair):
        uk, uv = uk_ref[n], uv_ref[n]
        rows = slice(n * tokens, (n + 1) * tokens)
        qct_ref[:latw, rows] = dot(uk, qt_ref[n, :nope]).astype(BF16)
        qct_ref[latw:, rows] = qt_ref[n, nope:]
        qc_ref[rows, :latw] = dot(qt_ref[n, :nope].T, uk, ((1,), (1,))).astype(BF16)
        qc_ref[rows, latw:] = qt_ref[n, nope:].T
        glt_ref[:, rows] = dot(uv, gt_ref[n]).astype(BF16)
        gl_ref[rows] = dot(gt_ref[n].T, uv, ((1,), (1,))).astype(BF16)
    shape = bias_ref.shape
    row = pl.program_id(0) * shape[0] + lax.broadcasted_iota(jnp.int32, shape, 0)
    kpos = info_ref[1] + row
    qpos = info_ref[1] + BACK * tokens + lax.broadcasted_iota(jnp.int32, shape, 1)
    visible = (kpos >= start_ref[...]) & (kpos <= qpos)
    bias_ref[...] = jnp.where(visible, 0.0, -jnp.inf).astype(F32)


def prepare(info, qt, gt, w_uk, w_uv, doc_start, pair=2):
    heads, qw, tokens = qt.shape
    latw, nope = w_uk.shape[1:]
    vdim = gt.shape[1]
    width = latw + qw - nope
    span = (BACK + 1) * tokens
    one = lambda *dims: pl.BlockSpec((pair, *dims), lambda h, s: (h, 0, 0))
    rows = lambda n, d: pl.BlockSpec((pair * n, d), lambda h, s: (h, 0))
    lanes = lambda d, n: pl.BlockSpec((d, pair * n), lambda h, s: (0, h))
    return pl.pallas_call(
        prepare_kernel,
        out_shape=(
            jax.ShapeDtypeStruct((width, heads * tokens), BF16),
            jax.ShapeDtypeStruct((heads * tokens, width), BF16),
            jax.ShapeDtypeStruct((latw, heads * tokens), BF16),
            jax.ShapeDtypeStruct((heads * tokens, latw), BF16),
            jax.ShapeDtypeStruct((span, tokens), F32),
        ),
        grid_spec=pltpu.PrefetchScalarGridSpec(
            num_scalar_prefetch=1,
            grid=(heads // pair,),
            in_specs=[
                one(qw, tokens), one(vdim, tokens), one(latw, nope), one(latw, vdim),
                pl.BlockSpec((1, tokens), lambda h, s: (0, 0)),
            ],
            out_specs=[
                lanes(width, tokens), rows(tokens, width), lanes(latw, tokens),
                rows(tokens, latw), rows(span // heads, tokens),
            ],
        ),
        compiler_params=pltpu.CompilerParams(vmem_limit_bytes=16 << 20),
        cost_estimate=pl.CostEstimate(
            flops=8 * heads * tokens * latw * nope, transcendentals=0,
            bytes_accessed=16 << 20,
        ),
        name="prepare",
    )(info, qt, gt, w_uk, w_uv, doc_start)


def join(block_ref, core, mine_ref, theirs_ref):
    rows = mine_ref.shape[0]
    block_ref[pl.ds(pl.multiple_of(core * rows, rows), rows)] = mine_ref[...]
    block_ref[pl.ds(pl.multiple_of((1 - core) * rows, rows), rows)] = theirs_ref[...]


def main_kernel(
    info_ref, start_ref, qct_ref, glt_ref, bias_ref, own_ref,
    m3_ref, m2_ref, m1_ref, t3_ref, t2_ref, t1_ref, qc_hbm, gl_hbm,
    ds_ref, keep_ref, send_ref,
    block_s, keys_s, expo_s, dprob_s, p_s, ds_s, qc_s, gl_s, sems, *, factor,
):
    step = pl.program_id(0)
    core = info_ref[0]
    span, tokens = bias_ref.shape
    low = jnp.maximum(start_ref[0] - info_ref[1], 0) // tokens
    latw, lanes = glt_ref.shape
    chunk = CHUNK * tokens // lanes
    scale = factor * math.log2(math.e)

    @pl.when(step == 0)
    def _():
        pltpu.make_async_copy(qc_hbm, qc_s, sems.at[0]).start()
        pltpu.make_async_copy(gl_hbm, gl_s, sems.at[1]).start()
        for block, (mine, theirs) in enumerate(
            ((m3_ref, t3_ref), (m2_ref, t2_ref), (m1_ref, t1_ref))
        ):
            join(block_s.at[block % 2], core, mine, theirs)
            keys_s[block * tokens : (block + 1) * tokens] = block_s[block % 2].T
        keys_s[BACK * tokens :] = own_ref[...].T

    def fold(x, op):
        return op(x.reshape(-1, 8, lanes), axis=0)

    def heads_from(begin):
        lane = pl.ds(pl.multiple_of(step * lanes, lanes), lanes)
        tops, totals = [], []
        for block in range(begin, span, tokens):
            scores = dot(keys_s[block : block + tokens], qct_ref[...])
            for c in range(0, tokens, chunk):
                at = slice(block + c, block + c + chunk)
                bias = jnp.concatenate([bias_ref[at]] * (lanes // tokens), 1)
                s = scores[c : c + chunk] * scale + bias
                top = jnp.max(fold(s, jnp.max), axis=0, keepdims=True)
                top = jnp.maximum(top, LOWEST)
                e = jnp.exp2(s - top)
                expo_s[at] = e
                tops.append(top)
                totals.append(jnp.sum(fold(e, jnp.sum), axis=0, keepdims=True))
        top = functools.reduce(jnp.maximum, tops)
        weights = [jnp.exp2(t - top) for t in tops]
        inverse = 1.0 / sum(w * t for w, t in zip(weights, totals))
        delta = jnp.zeros((8, lanes), F32)
        for block in range(begin, span, tokens):
            dprob = dot(keys_s[block : block + tokens, :latw], glt_ref[...])
            for c in range(0, tokens, chunk):
                at = slice(block + c, block + c + chunk)
                weight = weights[(block + c - begin) // chunk] * inverse
                p = (expo_s[at] * weight).astype(BF16)
                dp = dprob[c : c + chunk]
                p_s[at, lane] = p
                dprob_s[at] = dp
                delta = delta + fold(p.astype(F32) * dp, jnp.sum)
        delta = jnp.sum(delta, axis=0, keepdims=True)
        for c in range(begin, span, chunk):
            at = slice(c, c + chunk)
            ds = (p_s[at, lane].astype(F32) * (dprob_s[at] - delta)).astype(BF16)
            ds_s[at, lane] = ds
            ds_ref[at] = ds
        if begin:
            ds_ref[:begin] = jnp.zeros((begin, lanes), BF16)

    for block in range(BACK + 1):
        pl.when(low == block)(functools.partial(heads_from, block * tokens))

    @pl.when(step == pl.num_programs(0) - 1)
    def _():
        pltpu.make_async_copy(qc_hbm, qc_s, sems.at[0]).wait()
        pltpu.make_async_copy(gl_hbm, gl_s, sems.at[1]).wait()
        groups, piece = keep_ref.shape[1:3]

        def gradient(block, _):
            at = pl.ds(pl.multiple_of(block * tokens, tokens), tokens)

            def put(column, value):
                sides = value.reshape(groups, CORES, piece, -1)
                zeroth, first = sides[:, 0], sides[:, 1]
                keep_ref[block, :, :, column] = jnp.where(core == 0, zeroth, first).astype(BF16)
                send_ref[block, :, :, column] = jnp.where(core == 0, first, zeroth).astype(BF16)

            key = dot(ds_s[at], qc_s[...]) * factor
            put(slice(0, latw), key[:, :latw] + dot(p_s[at], gl_s[...]))
            put(slice(latw, None), key[:, latw:])
            return 0

        def blank(block, _):
            keep_ref[block] = jnp.zeros(keep_ref.shape[1:], BF16)
            send_ref[block] = jnp.zeros(send_ref.shape[1:], BF16)
            return 0

        lax.fori_loop(0, low, blank, 0)
        lax.fori_loop(low, BACK + 1, gradient, 0)


def attend(info, doc_start, qct, glt, bias, own, mine, theirs, qc, gl, factor, groups, pair=PAIR):
    width, queries = qct.shape
    latw = glt.shape[0]
    span, tokens = bias.shape
    lanes = pair * tokens
    piece = tokens // CORES // groups
    head = lambda d: pl.BlockSpec((d, lanes), lambda h, *_: (0, h))
    whole = lambda a: pl.BlockSpec(a.shape, lambda h, *_: (0,) * a.ndim)
    out = (BACK + 1, groups, piece, width)
    return pl.pallas_call(
        functools.partial(main_kernel, factor=factor),
        out_shape=(
            pltpu.HBM((span, queries), BF16),
            jax.ShapeDtypeStruct(out, BF16),
            jax.ShapeDtypeStruct(out, BF16),
        ),
        grid_spec=pltpu.PrefetchScalarGridSpec(
            num_scalar_prefetch=2,
            grid=(queries // lanes,),
            in_specs=[head(width), head(latw), whole(bias), whole(own)]
            + [whole(a) for a in (*mine, *theirs)]
            + [pl.BlockSpec(memory_space=pl.ANY)] * 2,
            out_specs=[
                head(span),
                pl.BlockSpec(out, lambda h, *_: (0, 0, 0, 0)),
                pl.BlockSpec(out, lambda h, *_: (0, 0, 0, 0)),
            ],
            scratch_shapes=[
                pltpu.VMEM((2, width, tokens), BF16),
                pltpu.VMEM((span, width), BF16),
                pltpu.VMEM((span, lanes), F32),
                pltpu.VMEM((span, lanes), F32),
                pltpu.VMEM((span, queries), BF16),
                pltpu.VMEM((span, queries), BF16),
                pltpu.VMEM(qc.shape, BF16),
                pltpu.VMEM(gl.shape, BF16),
                pltpu.SemaphoreType.DMA((2,)),
            ],
        ),
        compiler_params=pltpu.CompilerParams(vmem_limit_bytes=38 << 20),
        cost_estimate=pl.CostEstimate(
            flops=4 * queries * span * (width + latw),
            transcendentals=queries * span, bytes_accessed=24 << 20,
        ),
        name="attend",
    )(info, doc_start, qct, glt, bias, own, *mine, *theirs, qc, gl)


def query_kernel(
    info_ref, ds_ref, uk_ref, own_ref, m3_ref, m2_ref, m1_ref, t3_ref, t2_ref, t1_ref,
    out_ref, keys_s, *, factor,
):
    core = info_ref[0]
    tokens = own_ref.shape[1]
    pair, latw, nope = uk_ref.shape

    @pl.when(pl.program_id(0) == 0)
    def _():
        for block, (mine, theirs) in enumerate(
            ((m3_ref, t3_ref), (m2_ref, t2_ref), (m1_ref, t1_ref))
        ):
            join(keys_s.at[:, pl.ds(block * tokens, tokens)], core, mine, theirs)
        keys_s[:, BACK * tokens :] = own_ref[...]

    all_dq = dot(keys_s[...], ds_ref[...]) * factor
    for n in range(pair):
        dq = all_dq[:, n * tokens : (n + 1) * tokens]
        dq_nope = dot(uk_ref[n], dq[:latw].astype(BF16), ((0,), (0,)))
        out_ref[n, :nope] = dq_nope.astype(BF16)
        out_ref[n, nope:] = dq[latw:].astype(BF16)


def query_gradient(info, ds, w_uk, own, mine, theirs, factor, pair=4):
    span = ds.shape[0]
    heads, latw, nope = w_uk.shape
    width, tokens = own.shape
    qw = nope + width - latw
    whole = lambda a: pl.BlockSpec(a.shape, lambda h, s: (0,) * a.ndim)
    return pl.pallas_call(
        functools.partial(query_kernel, factor=factor),
        out_shape=jax.ShapeDtypeStruct((heads, qw, tokens), BF16),
        grid_spec=pltpu.PrefetchScalarGridSpec(
            num_scalar_prefetch=1,
            grid=(heads // pair,),
            in_specs=[
                pl.BlockSpec((span, pair * tokens), lambda h, s: (0, h)),
                pl.BlockSpec((pair, latw, nope), lambda h, s: (h, 0, 0)),
                whole(own),
            ]
            + [whole(a) for a in (*mine, *theirs)],
            out_specs=pl.BlockSpec((pair, qw, tokens), lambda h, s: (h, 0, 0)),
            scratch_shapes=[pltpu.VMEM((width, span), BF16)],
        ),
        compiler_params=pltpu.CompilerParams(vmem_limit_bytes=24 << 20),
        cost_estimate=pl.CostEstimate(
            flops=2 * heads * tokens * (span * width + latw * nope),
            transcendentals=0, bytes_accessed=8 << 20,
        ),
        name="query_gradient",
    )(info, ds, w_uk, own, *mine, *theirs)


def along_seq(distance, crossings=True):
    devices = lax.axis_size("seq")
    pairs = []
    for source in range(devices):
        target = source + distance
        if 0 <= target < devices:
            crossing = (2 * source < devices) != (2 * target < devices)
            if crossings or not crossing:
                pairs += between(source, target, crossing)
    return pairs


def between(source, target, turned=False):
    heads = lax.axis_size("head")
    pairs = []
    for head in range(heads):
        chip, core = divmod(head, CORES)
        if turned:
            chip ^= heads // CORES // 2
        pairs.append((source * heads + head, target * heads + chip * CORES + core))
    return pairs


def send(value, pairs):
    return lax.ppermute(value, ("seq", "head"), pairs)


def in_hbm(value):
    return pltpu.with_memory_space_constraint(value, pltpu.HBM)


def swap_cores(value):
    return lax.ppermute(value, "head", [(k, k ^ 1) for k in range(lax.axis_size("head"))])


def shards(queries, grad_out, latent, w_uk, w_uv, doc_start):
    tokens, width = latent.shape
    factor = queries.shape[2] ** (-0.5)
    seq, head = lax.axis_index("seq"), lax.axis_index("head")
    heads = lax.axis_size("head")
    chips = heads // CORES
    core, chip = head % CORES, head // CORES
    half = width // CORES

    own = latent.T
    part = lax.dynamic_slice_in_dim(own, core * half, half, 0)
    far = send(part, along_seq(3))
    near = [send(part, along_seq(distance, False)) for distance in (2, 1)]

    middle = lax.axis_size("seq") // 2
    after, next_one, next_two = middle, middle + 1, middle + 2
    relays = (between(next_one, after) + between(next_two, next_one), between(next_two, after))

    info = jnp.stack([core, (seq - BACK) * tokens]).astype(jnp.int32)
    qt = jnp.transpose(queries, (1, 2, 0))
    gt = jnp.transpose(grad_out, (1, 2, 0))
    far, gt = lax.optimization_barrier((far, gt))
    relayed = [send(far, relay) for relay in relays]
    prepared = prepare(
        info, in_hbm(qt), gt, in_hbm(w_uk), in_hbm(w_uv), in_hbm(doc_start[None])
    )
    near, relayed, prepared = lax.optimization_barrier((near[::-1], relayed, prepared))
    qct, qc, glt, gl, bias = prepared
    mine = [far] + [direct + other for direct, other in zip(near[::-1], relayed)]
    theirs = [swap_cores(piece) for piece in mine]

    ds, keep, away = attend(
        info, doc_start, qct, glt, bias, own, mine, theirs, qc, gl, factor, chips
    )
    both = keep + swap_cores(away)
    kept, gone = halve(both, 1, chip, 1)
    both = kept.astype(F32) + trade(gone, 1).astype(F32)
    *far, total = list(both)
    back = [
        send(far[BACK - distance].astype(BF16), along_seq(-distance))
        for distance in range(1, BACK + 1)
    ]
    dq = query_gradient(info, in_hbm(ds), in_hbm(w_uk), own, mine, theirs, factor)
    back, dq = lax.optimization_barrier((back, dq))
    for piece in back:
        total = total + piece.astype(F32)
    bit = 2
    while bit < chips:
        kept, gone = halve(total, 0, chip, bit)
        total = kept + trade(gone.astype(BF16), bit).astype(F32)
        bit *= 2
    grad_query = jnp.transpose(dq, (2, 0, 1))
    return grad_query, total[0]


def halve(value, dim, chip, bit):
    lengths = value.shape
    halves = value.reshape(*lengths[:dim], lengths[dim] // 2, 2, *lengths[dim + 1 :])
    mine = chip // bit % 2
    return (
        lax.dynamic_index_in_dim(halves, mine, dim + 1, False),
        lax.dynamic_index_in_dim(halves, 1 - mine, dim + 1, False),
    )


def trade(value, bit):
    route = [(k, k ^ (bit * CORES)) for k in range(lax.axis_size("head"))]
    return lax.ppermute(value, "head", route)


def solution(mesh):
    placed = (
        P("seq", "head", None),
        P("seq", "head", None),
        P("seq", None),
        P("head", None, None),
        P("head", None, None),
        P("seq"),
    )
    return jax.shard_map(
        shards,
        mesh=mesh,
        in_specs=placed,
        out_specs=(P("seq", "head", None), P(("seq", "head"), None)),
        check_vma=False,
    )
```

```python
import functools
import math

import jax
import jax.numpy as jnp
from jax import lax
from jax.experimental import pallas as pl
from jax.experimental.pallas import tpu as pltpu
from jax.sharding import PartitionSpec as P

BACK = 3
CORES = 2
BF16 = jnp.bfloat16
F32 = jnp.float32


def dot(a, b, contract=((1,), (0,))):
    return lax.dot_general(a, b, (contract, ((), ())), preferred_element_type=F32)


LOWEST = -1e30
CHUNK = 64
PAIR = 1
LIMIT = 32


def prepare_kernel(
    info_ref, qt_ref, gt_ref, uk_ref, uv_ref, start_ref,
    qct_ref, qc_ref, glt_ref, gl_ref, bias_ref,
):
    pair, latw, nope = uk_ref.shape
    tokens = qt_ref.shape[2]
    for n in range(pair):
        uk, uv = uk_ref[n], uv_ref[n]
        rows = slice(n * tokens, (n + 1) * tokens)
        qct_ref[:latw, rows] = dot(uk, qt_ref[n, :nope]).astype(BF16)
        qct_ref[latw:, rows] = qt_ref[n, nope:]
        qc_ref[rows, :latw] = dot(qt_ref[n, :nope].T, uk, ((1,), (1,))).astype(BF16)
        qc_ref[rows, latw:] = qt_ref[n, nope:].T
        glt_ref[:, rows] = dot(uv, gt_ref[n]).astype(BF16)
        gl_ref[rows] = dot(gt_ref[n].T, uv, ((1,), (1,))).astype(BF16)
    shape = bias_ref.shape
    row = pl.program_id(0) * shape[0] + lax.broadcasted_iota(jnp.int32, shape, 0)
    kpos = info_ref[1] + row
    qpos = info_ref[1] + BACK * tokens + lax.broadcasted_iota(jnp.int32, shape, 1)
    visible = (kpos >= start_ref[...]) & (kpos <= qpos)
    bias_ref[...] = jnp.where(visible, 0.0, -jnp.inf).astype(F32)


def prepare(info, qt, gt, w_uk, w_uv, doc_start, pair=2):
    heads, qw, tokens = qt.shape
    latw, nope = w_uk.shape[1:]
    vdim = gt.shape[1]
    width = latw + qw - nope
    span = (BACK + 1) * tokens
    one = lambda *dims: pl.BlockSpec((pair, *dims), lambda h, s: (h, 0, 0))
    rows = lambda n, d: pl.BlockSpec((pair * n, d), lambda h, s: (h, 0))
    lanes = lambda d, n: pl.BlockSpec((d, pair * n), lambda h, s: (0, h))
    return pl.pallas_call(
        prepare_kernel,
        out_shape=(
            jax.ShapeDtypeStruct((width, heads * tokens), BF16),
            jax.ShapeDtypeStruct((heads * tokens, width), BF16),
            jax.ShapeDtypeStruct((latw, heads * tokens), BF16),
            jax.ShapeDtypeStruct((heads * tokens, latw), BF16),
            jax.ShapeDtypeStruct((span, tokens), F32),
        ),
        grid_spec=pltpu.PrefetchScalarGridSpec(
            num_scalar_prefetch=1,
            grid=(heads // pair,),
            in_specs=[
                one(qw, tokens), one(vdim, tokens), one(latw, nope), one(latw, vdim),
                pl.BlockSpec((1, tokens), lambda h, s: (0, 0)),
            ],
            out_specs=[
                lanes(width, tokens), rows(tokens, width), lanes(latw, tokens),
                rows(tokens, latw), rows(span // heads, tokens),
            ],
        ),
        compiler_params=pltpu.CompilerParams(vmem_limit_bytes=16 << 20),
        cost_estimate=pl.CostEstimate(
            flops=8 * heads * tokens * latw * nope, transcendentals=0,
            bytes_accessed=16 << 20,
        ),
        name="prepare",
    )(info, qt, gt, w_uk, w_uv, doc_start)


def join(block_ref, core, mine_ref, theirs_ref):
    rows = mine_ref.shape[0]
    block_ref[pl.ds(pl.multiple_of(core * rows, rows), rows)] = mine_ref[...]
    block_ref[pl.ds(pl.multiple_of((1 - core) * rows, rows), rows)] = theirs_ref[...]


def main_kernel(
    info_ref, start_ref, qct_ref, glt_ref, bias_ref, own_ref,
    m3_ref, m2_ref, m1_ref, t3_ref, t2_ref, t1_ref, qc_ref, gl_ref,
    ds_hbm, keep_ref, send_ref,
    block_s, keys_s, expo_s, dprob_s, p_s, ds_s, sems, *, factor, pair,
):
    core = info_ref[0]
    span, tokens = bias_ref.shape
    low = jnp.maximum(start_ref[0] - info_ref[1], 0) // tokens
    latw, queries = glt_ref.shape
    lanes = pair * tokens
    steps = queries // lanes
    chunk = CHUNK // pair
    scale = factor * math.log2(math.e)

    for block, (mine, theirs) in enumerate(
        ((m3_ref, t3_ref), (m2_ref, t2_ref), (m1_ref, t1_ref))
    ):
        join(block_s.at[block % 2], core, mine, theirs)
        keys_s[block * tokens : (block + 1) * tokens] = block_s[block % 2].T
    keys_s[BACK * tokens :] = own_ref[...].T

    def fold(x, op):
        return op(x.reshape(-1, 8, lanes), axis=0)

    def store_ds(step):
        lane = slice(step * lanes, (step + 1) * lanes)
        return pltpu.make_async_copy(ds_s.at[:, lane], ds_hbm.at[:, lane], sems.at[step])

    def heads_from(begin, step):
        lane = slice(step * lanes, (step + 1) * lanes)
        slot = step % 2
        tops, totals = [], []
        for block in range(begin, span, tokens):
            scores = dot(keys_s[block : block + tokens], qct_ref[:, lane])
            for c in range(0, tokens, chunk):
                at = slice(block + c, block + c + chunk)
                bias = jnp.concatenate([bias_ref[at]] * (lanes // tokens), 1)
                s = scores[c : c + chunk] * scale + bias
                top = jnp.max(fold(s, jnp.max), axis=0, keepdims=True)
                top = jnp.maximum(top, LOWEST)
                e = jnp.exp2(s - top)
                expo_s[slot, at] = e
                tops.append(top)
                totals.append(jnp.sum(fold(e, jnp.sum), axis=0, keepdims=True))
        top = functools.reduce(jnp.maximum, tops)
        weights = [jnp.exp2(t - top) for t in tops]
        inverse = 1.0 / sum(w * t for w, t in zip(weights, totals))
        delta = jnp.zeros((8, lanes), F32)
        for block in range(begin, span, tokens):
            dprob = dot(keys_s[block : block + tokens, :latw], glt_ref[:, lane])
            for c in range(0, tokens, chunk):
                at = slice(block + c, block + c + chunk)
                weight = weights[(block + c - begin) // chunk] * inverse
                p = (expo_s[slot, at] * weight).astype(BF16)
                dp = dprob[c : c + chunk]
                p_s[at, lane] = p
                dprob_s[slot, at] = dp
                delta = delta + fold(p.astype(F32) * dp, jnp.sum)
        delta = jnp.sum(delta, axis=0, keepdims=True)
        for c in range(begin, span, chunk):
            at = slice(c, c + chunk)
            ds = (p_s[at, lane].astype(F32) * (dprob_s[slot, at] - delta)).astype(BF16)
            ds_s[at, lane] = ds
        if begin:
            ds_s[:begin, lane] = jnp.zeros((begin, lanes), BF16)
        store_ds(step).start()

    def all_heads_from(begin):
        for step in range(steps):
            heads_from(begin, step)

    for block in range(BACK + 1):
        pl.when(low == block)(functools.partial(all_heads_from, block * tokens))
    groups, piece = keep_ref.shape[1:3]

    def gradient(block, _):
        at = pl.ds(pl.multiple_of(block * tokens, tokens), tokens)

        def put(column, value):
            sides = value.reshape(groups, CORES, piece, -1)
            zeroth, first = sides[:, 0], sides[:, 1]
            keep_ref[block, :, :, column] = jnp.where(core == 0, zeroth, first).astype(BF16)
            send_ref[block, :, :, column] = jnp.where(core == 0, first, zeroth).astype(BF16)

        key = dot(ds_s[at], qc_ref[...]) * factor
        put(slice(0, latw), key[:, :latw] + dot(p_s[at], gl_ref[...]))
        put(slice(latw, None), key[:, latw:])
        return 0

    def blank(block, _):
        keep_ref[block] = jnp.zeros(keep_ref.shape[1:], BF16)
        send_ref[block] = jnp.zeros(send_ref.shape[1:], BF16)
        return 0

    lax.fori_loop(0, low, blank, 0)
    lax.fori_loop(low, BACK + 1, gradient, 0)
    for step in range(steps):
        store_ds(step).wait()


def attend(info, doc_start, qct, glt, bias, own, mine, theirs, qc, gl, factor, groups, pair=PAIR):
    width, queries = qct.shape
    latw = glt.shape[0]
    span, tokens = bias.shape
    piece = tokens // CORES // groups
    out = (BACK + 1, groups, piece, width)
    scalars = pl.BlockSpec(memory_space=pltpu.SMEM)
    onchip = pl.BlockSpec(memory_space=pltpu.VMEM)
    operands = [qct, glt, bias, own, *mine, *theirs, qc, gl]
    return pl.pallas_call(
        functools.partial(main_kernel, factor=factor, pair=pair),
        out_shape=(
            pltpu.HBM((span, queries), BF16),
            jax.ShapeDtypeStruct(out, BF16),
            jax.ShapeDtypeStruct(out, BF16),
        ),
        in_specs=[scalars, scalars] + [onchip] * len(operands),
        out_specs=[pl.BlockSpec(memory_space=pl.ANY), onchip, onchip],
        scratch_shapes=[
            pltpu.VMEM((2, width, tokens), BF16),
            pltpu.VMEM((span, width), BF16),
            pltpu.VMEM((2, span, pair * tokens), F32),
            pltpu.VMEM((2, span, pair * tokens), F32),
            pltpu.VMEM((span, queries), BF16),
            pltpu.VMEM((span, queries), BF16),
            pltpu.SemaphoreType.DMA((queries // tokens // pair,)),
        ],
        compiler_params=pltpu.CompilerParams(vmem_limit_bytes=LIMIT << 20),
        cost_estimate=pl.CostEstimate(
            flops=4 * queries * span * (width + latw),
            transcendentals=queries * span, bytes_accessed=24 << 20,
        ),
        name="attend",
    )(info, doc_start, *operands)


def query_kernel(
    info_ref, ds_ref, uk_ref, own_ref, m3_ref, m2_ref, m1_ref, t3_ref, t2_ref, t1_ref,
    out_ref, keys_s, *, factor,
):
    core = info_ref[0]
    tokens = own_ref.shape[1]
    pair, latw, nope = uk_ref.shape

    @pl.when(pl.program_id(0) == 0)
    def _():
        for block, (mine, theirs) in enumerate(
            ((m3_ref, t3_ref), (m2_ref, t2_ref), (m1_ref, t1_ref))
        ):
            join(keys_s.at[:, pl.ds(block * tokens, tokens)], core, mine, theirs)
        keys_s[:, BACK * tokens :] = own_ref[...]

    all_dq = dot(keys_s[...], ds_ref[...]) * factor
    for n in range(pair):
        dq = all_dq[:, n * tokens : (n + 1) * tokens]
        dq_nope = dot(uk_ref[n], dq[:latw].astype(BF16), ((0,), (0,)))
        out_ref[n, :nope] = dq_nope.astype(BF16)
        out_ref[n, nope:] = dq[latw:].astype(BF16)


def query_gradient(info, ds, w_uk, own, mine, theirs, factor, pair=4):
    span = ds.shape[0]
    heads, latw, nope = w_uk.shape
    width, tokens = own.shape
    qw = nope + width - latw
    whole = lambda a: pl.BlockSpec(a.shape, lambda h, s: (0,) * a.ndim)
    return pl.pallas_call(
        functools.partial(query_kernel, factor=factor),
        out_shape=jax.ShapeDtypeStruct((heads, qw, tokens), BF16),
        grid_spec=pltpu.PrefetchScalarGridSpec(
            num_scalar_prefetch=1,
            grid=(heads // pair,),
            in_specs=[
                pl.BlockSpec((span, pair * tokens), lambda h, s: (0, h)),
                pl.BlockSpec((pair, latw, nope), lambda h, s: (h, 0, 0)),
                whole(own),
            ]
            + [whole(a) for a in (*mine, *theirs)],
            out_specs=pl.BlockSpec((pair, qw, tokens), lambda h, s: (h, 0, 0)),
            scratch_shapes=[pltpu.VMEM((width, span), BF16)],
        ),
        compiler_params=pltpu.CompilerParams(vmem_limit_bytes=24 << 20),
        cost_estimate=pl.CostEstimate(
            flops=2 * heads * tokens * (span * width + latw * nope),
            transcendentals=0, bytes_accessed=8 << 20,
        ),
        name="query_gradient",
    )(info, ds, w_uk, own, *mine, *theirs)


def along_seq(distance, crossings=True):
    devices = lax.axis_size("seq")
    pairs = []
    for source in range(devices):
        target = source + distance
        if 0 <= target < devices:
            crossing = (2 * source < devices) != (2 * target < devices)
            if crossings or not crossing:
                pairs += between(source, target, crossing)
    return pairs


def between(source, target, turned=False):
    heads = lax.axis_size("head")
    pairs = []
    for head in range(heads):
        chip, core = divmod(head, CORES)
        if turned:
            chip ^= heads // CORES // 2
        pairs.append((source * heads + head, target * heads + chip * CORES + core))
    return pairs


def send(value, pairs):
    return lax.ppermute(value, ("seq", "head"), pairs)


def in_hbm(value):
    return pltpu.with_memory_space_constraint(value, pltpu.HBM)


def swap_cores(value):
    return lax.ppermute(value, "head", [(k, k ^ 1) for k in range(lax.axis_size("head"))])


def shards(queries, grad_out, latent, w_uk, w_uv, doc_start):
    tokens, width = latent.shape
    factor = queries.shape[2] ** (-0.5)
    seq, head = lax.axis_index("seq"), lax.axis_index("head")
    heads = lax.axis_size("head")
    chips = heads // CORES
    core, chip = head % CORES, head // CORES
    half = width // CORES

    own = latent.T
    part = lax.dynamic_slice_in_dim(own, core * half, half, 0)
    far = send(part, along_seq(3))
    near = [send(part, along_seq(distance, False)) for distance in (2, 1)]

    middle = lax.axis_size("seq") // 2
    after, next_one, next_two = middle, middle + 1, middle + 2
    relays = (between(next_one, after) + between(next_two, next_one), between(next_two, after))

    info = jnp.stack([core, (seq - BACK) * tokens]).astype(jnp.int32)
    qt = jnp.transpose(queries, (1, 2, 0))
    gt = jnp.transpose(grad_out, (1, 2, 0))
    far, gt = lax.optimization_barrier((far, gt))
    relayed = [send(far, relay) for relay in relays]
    prepared = prepare(
        info, in_hbm(qt), gt, in_hbm(w_uk), in_hbm(w_uv), in_hbm(doc_start[None])
    )
    near, relayed, prepared = lax.optimization_barrier((near[::-1], relayed, prepared))
    qct, qc, glt, gl, bias = prepared
    mine = [far] + [direct + other for direct, other in zip(near[::-1], relayed)]
    theirs = [swap_cores(piece) for piece in mine]

    ds, keep, away = attend(
        info, doc_start, qct, glt, bias, own, mine, theirs, qc, gl, factor, chips
    )
    both = keep + swap_cores(away)
    kept, gone = halve(both, 1, chip, 1)
    gone, ds = lax.optimization_barrier((gone, ds))
    arrived = trade(gone, 1)
    dq = query_gradient(info, in_hbm(ds), in_hbm(w_uk), own, mine, theirs, factor)
    arrived, dq = lax.optimization_barrier((arrived, dq))
    both = kept.astype(F32) + arrived.astype(F32)
    *far, total = list(both)
    back = [
        send(far[BACK - distance].astype(BF16), along_seq(-distance))
        for distance in range(1, BACK + 1)
    ]
    for piece in back:
        total = total + piece.astype(F32)
    bit = 2
    while bit < chips:
        kept, gone = halve(total, 0, chip, bit)
        total = kept + trade(gone.astype(BF16), bit).astype(F32)
        bit *= 2
    grad_query = jnp.transpose(dq, (2, 0, 1))
    return grad_query, total[0]


def halve(value, dim, chip, bit):
    lengths = value.shape
    halves = value.reshape(*lengths[:dim], lengths[dim] // 2, 2, *lengths[dim + 1 :])
    mine = chip // bit % 2
    return (
        lax.dynamic_index_in_dim(halves, mine, dim + 1, False),
        lax.dynamic_index_in_dim(halves, 1 - mine, dim + 1, False),
    )


def trade(value, bit):
    route = [(k, k ^ (bit * CORES)) for k in range(lax.axis_size("head"))]
    return lax.ppermute(value, "head", route)


def solution(mesh):
    placed = (
        P("seq", "head", None),
        P("seq", "head", None),
        P("seq", None),
        P("head", None, None),
        P("head", None, None),
        P("seq"),
    )
    return jax.shard_map(
        shards,
        mesh=mesh,
        in_specs=placed,
        out_specs=(P("seq", "head", None), P(("seq", "head"), None)),
        check_vma=False,
    )
```

```python
import functools
import math

import jax
import jax.numpy as jnp
from jax import lax
from jax.experimental import pallas as pl
from jax.experimental.pallas import tpu as pltpu
from jax.sharding import PartitionSpec as P

BACK = 3
CORES = 2
BF16 = jnp.bfloat16
F32 = jnp.float32


def dot(a, b, contract=((1,), (0,))):
    return lax.dot_general(a, b, (contract, ((), ())), preferred_element_type=F32)


LOWEST = -1e30
CHUNK = 128
PAIR = 1
LIMIT = 32


def prepare_kernel(
    info_ref, qt_ref, gt_ref, uk_ref, uv_ref, start_ref,
    qct_ref, qc_ref, glt_ref, gl_ref, bias_ref,
):
    pair, latw, nope = uk_ref.shape
    tokens = qt_ref.shape[2]
    for n in range(pair):
        uk, uv = uk_ref[n], uv_ref[n]
        rows = slice(n * tokens, (n + 1) * tokens)
        qct_ref[:latw, rows] = dot(uk, qt_ref[n, :nope]).astype(BF16)
        qct_ref[latw:, rows] = qt_ref[n, nope:]
        qc_ref[rows, :latw] = dot(qt_ref[n, :nope].T, uk, ((1,), (1,))).astype(BF16)
        qc_ref[rows, latw:] = qt_ref[n, nope:].T
        glt_ref[:, rows] = dot(uv, gt_ref[n]).astype(BF16)
        gl_ref[rows] = dot(gt_ref[n].T, uv, ((1,), (1,))).astype(BF16)
    shape = bias_ref.shape
    row = pl.program_id(0) * shape[0] + lax.broadcasted_iota(jnp.int32, shape, 0)
    kpos = info_ref[1] + row
    qpos = info_ref[1] + BACK * tokens + lax.broadcasted_iota(jnp.int32, shape, 1)
    visible = (kpos >= start_ref[...]) & (kpos <= qpos)
    bias_ref[...] = jnp.where(visible, 0.0, -jnp.inf).astype(F32)


def prepare(info, qt, gt, w_uk, w_uv, doc_start, pair=2):
    heads, qw, tokens = qt.shape
    latw, nope = w_uk.shape[1:]
    vdim = gt.shape[1]
    width = latw + qw - nope
    span = (BACK + 1) * tokens
    one = lambda *dims: pl.BlockSpec((pair, *dims), lambda h, s: (h, 0, 0))
    rows = lambda n, d: pl.BlockSpec((pair * n, d), lambda h, s: (h, 0))
    lanes = lambda d, n: pl.BlockSpec((d, pair * n), lambda h, s: (0, h))
    return pl.pallas_call(
        prepare_kernel,
        out_shape=(
            jax.ShapeDtypeStruct((width, heads * tokens), BF16),
            jax.ShapeDtypeStruct((heads * tokens, width), BF16),
            jax.ShapeDtypeStruct((latw, heads * tokens), BF16),
            jax.ShapeDtypeStruct((heads * tokens, latw), BF16),
            jax.ShapeDtypeStruct((span, tokens), F32),
        ),
        grid_spec=pltpu.PrefetchScalarGridSpec(
            num_scalar_prefetch=1,
            grid=(heads // pair,),
            in_specs=[
                one(qw, tokens), one(vdim, tokens), one(latw, nope), one(latw, vdim),
                pl.BlockSpec((1, tokens), lambda h, s: (0, 0)),
            ],
            out_specs=[
                lanes(width, tokens), rows(tokens, width), lanes(latw, tokens),
                rows(tokens, latw), rows(span // heads, tokens),
            ],
        ),
        compiler_params=pltpu.CompilerParams(vmem_limit_bytes=16 << 20),
        cost_estimate=pl.CostEstimate(
            flops=8 * heads * tokens * latw * nope, transcendentals=0,
            bytes_accessed=16 << 20,
        ),
        name="prepare",
    )(info, qt, gt, w_uk, w_uv, doc_start)


def join(block_ref, core, mine_ref, theirs_ref):
    rows = mine_ref.shape[0]
    block_ref[pl.ds(pl.multiple_of(core * rows, rows), rows)] = mine_ref[...]
    block_ref[pl.ds(pl.multiple_of((1 - core) * rows, rows), rows)] = theirs_ref[...]


def main_kernel(
    info_ref, start_ref, qct_ref, glt_ref, bias_ref, own_ref,
    m3_ref, m2_ref, m1_ref, t3_ref, t2_ref, t1_ref, qc_ref, gl_ref,
    ds_hbm, keep_ref, send_ref,
    block_s, keys_s, expo_s, dprob_s, p_s, ds_s, sems, *, factor, pair,
):
    core = info_ref[0]
    span, tokens = bias_ref.shape
    low = jnp.maximum(start_ref[0] - info_ref[1], 0) // tokens
    latw, queries = glt_ref.shape
    lanes = pair * tokens
    steps = queries // lanes
    chunk = CHUNK // pair
    scale = factor * math.log2(math.e)

    for block, (mine, theirs) in enumerate(
        ((m3_ref, t3_ref), (m2_ref, t2_ref), (m1_ref, t1_ref))
    ):
        join(block_s.at[block % 2], core, mine, theirs)
        keys_s[block * tokens : (block + 1) * tokens] = block_s[block % 2].T
    keys_s[BACK * tokens :] = own_ref[...].T

    def fold(x, op):
        return op(x.reshape(-1, 8, lanes), axis=0)

    def store_ds(step):
        lane = slice(step * lanes, (step + 1) * lanes)
        return pltpu.make_async_copy(ds_s.at[:, lane], ds_hbm.at[:, lane], sems.at[step])

    def heads_from(begin, step):
        lane = slice(step * lanes, (step + 1) * lanes)
        slot = step % 2
        tops, totals = [], []
        for block in range(begin, span, tokens):
            scores = dot(keys_s[block : block + tokens], qct_ref[:, lane])
            for c in range(0, tokens, chunk):
                at = slice(block + c, block + c + chunk)
                bias = jnp.concatenate([bias_ref[at]] * (lanes // tokens), 1)
                s = scores[c : c + chunk] * scale + bias
                top = jnp.max(fold(s, jnp.max), axis=0, keepdims=True)
                top = jnp.maximum(top, LOWEST)
                e = jnp.exp2(s - top)
                expo_s[slot, at] = e
                tops.append(top)
                totals.append(jnp.sum(fold(e, jnp.sum), axis=0, keepdims=True))
        top = functools.reduce(jnp.maximum, tops)
        weights = [jnp.exp2(t - top) for t in tops]
        inverse = 1.0 / sum(w * t for w, t in zip(weights, totals))
        delta = jnp.zeros((8, lanes), F32)
        for block in range(begin, span, tokens):
            dprob = dot(keys_s[block : block + tokens, :latw], glt_ref[:, lane])
            for c in range(0, tokens, chunk):
                at = slice(block + c, block + c + chunk)
                weight = weights[(block + c - begin) // chunk] * inverse
                p = (expo_s[slot, at] * weight).astype(BF16)
                dp = dprob[c : c + chunk]
                p_s[at, lane] = p
                dprob_s[slot, at] = dp
                delta = delta + fold(p.astype(F32) * dp, jnp.sum)
        delta = jnp.sum(delta, axis=0, keepdims=True)
        for c in range(begin, span, chunk):
            at = slice(c, c + chunk)
            ds = (p_s[at, lane].astype(F32) * (dprob_s[slot, at] - delta)).astype(BF16)
            ds_s[at, lane] = ds
        if begin:
            ds_s[:begin, lane] = jnp.zeros((begin, lanes), BF16)
        store_ds(step).start()

    def all_heads_from(begin):
        for step in range(steps):
            heads_from(begin, step)

    for block in range(BACK + 1):
        pl.when(low == block)(functools.partial(all_heads_from, block * tokens))
    groups, piece = keep_ref.shape[1:3]

    def gradient(low_block):
        def put(column, value):
            sides = value.reshape(-1, groups, CORES, piece, value.shape[1])
            zeroth, first = sides[:, :, 0], sides[:, :, 1]
            keep_ref[low_block:, :, :, column] = jnp.where(core == 0, zeroth, first).astype(BF16)
            send_ref[low_block:, :, :, column] = jnp.where(core == 0, first, zeroth).astype(BF16)

        begin = low_block * tokens
        key = dot(ds_s[begin:], qc_ref[...]) * factor
        put(slice(0, latw), key[:, :latw] + dot(p_s[begin:], gl_ref[...]))
        put(slice(latw, None), key[:, latw:])
        if low_block:
            shape = (low_block, *keep_ref.shape[1:])
            keep_ref[:low_block] = jnp.zeros(shape, BF16)
            send_ref[:low_block] = jnp.zeros(shape, BF16)

    for block in range(BACK + 1):
        pl.when(low == block)(functools.partial(gradient, block))

    for step in range(steps):
        store_ds(step).wait()


def attend(info, doc_start, qct, glt, bias, own, mine, theirs, qc, gl, factor, groups, pair=PAIR):
    width, queries = qct.shape
    latw = glt.shape[0]
    span, tokens = bias.shape
    piece = tokens // CORES // groups
    out = (BACK + 1, groups, piece, width)
    scalars = pl.BlockSpec(memory_space=pltpu.SMEM)
    onchip = pl.BlockSpec(memory_space=pltpu.VMEM)
    operands = [qct, glt, bias, own, *mine, *theirs, qc, gl]
    return pl.pallas_call(
        functools.partial(main_kernel, factor=factor, pair=pair),
        out_shape=(
            pltpu.HBM((span, queries), BF16),
            jax.ShapeDtypeStruct(out, BF16),
            jax.ShapeDtypeStruct(out, BF16),
        ),
        in_specs=[scalars, scalars] + [onchip] * len(operands),
        out_specs=[pl.BlockSpec(memory_space=pl.ANY), onchip, onchip],
        scratch_shapes=[
            pltpu.VMEM((2, width, tokens), BF16),
            pltpu.VMEM((span, width), BF16),
            pltpu.VMEM((2, span, pair * tokens), F32),
            pltpu.VMEM((2, span, pair * tokens), F32),
            pltpu.VMEM((span, queries), BF16),
            pltpu.VMEM((span, queries), BF16),
            pltpu.SemaphoreType.DMA((queries // tokens // pair,)),
        ],
        compiler_params=pltpu.CompilerParams(vmem_limit_bytes=LIMIT << 20),
        cost_estimate=pl.CostEstimate(
            flops=4 * queries * span * (width + latw),
            transcendentals=queries * span, bytes_accessed=24 << 20,
        ),
        name="attend",
    )(info, doc_start, *operands)


def query_kernel(
    info_ref, ds_ref, uk_ref, own_ref, m3_ref, m2_ref, m1_ref, t3_ref, t2_ref, t1_ref,
    out_ref, keys_s, *, factor,
):
    core = info_ref[0]
    tokens = own_ref.shape[1]
    pair, latw, nope = uk_ref.shape

    @pl.when(pl.program_id(0) == 0)
    def _():
        for block, (mine, theirs) in enumerate(
            ((m3_ref, t3_ref), (m2_ref, t2_ref), (m1_ref, t1_ref))
        ):
            join(keys_s.at[:, pl.ds(block * tokens, tokens)], core, mine, theirs)
        keys_s[:, BACK * tokens :] = own_ref[...]

    all_dq = dot(keys_s[...], ds_ref[...]) * factor
    for n in range(pair):
        dq = all_dq[:, n * tokens : (n + 1) * tokens]
        dq_nope = dot(uk_ref[n], dq[:latw].astype(BF16), ((0,), (0,)))
        out_ref[n, :nope] = dq_nope.astype(BF16)
        out_ref[n, nope:] = dq[latw:].astype(BF16)


def query_gradient(info, ds, w_uk, own, mine, theirs, factor, pair=4):
    span = ds.shape[0]
    heads, latw, nope = w_uk.shape
    width, tokens = own.shape
    qw = nope + width - latw
    whole = lambda a: pl.BlockSpec(a.shape, lambda h, s: (0,) * a.ndim)
    return pl.pallas_call(
        functools.partial(query_kernel, factor=factor),
        out_shape=jax.ShapeDtypeStruct((heads, qw, tokens), BF16),
        grid_spec=pltpu.PrefetchScalarGridSpec(
            num_scalar_prefetch=1,
            grid=(heads // pair,),
            in_specs=[
                pl.BlockSpec((span, pair * tokens), lambda h, s: (0, h)),
                pl.BlockSpec((pair, latw, nope), lambda h, s: (h, 0, 0)),
                whole(own),
            ]
            + [whole(a) for a in (*mine, *theirs)],
            out_specs=pl.BlockSpec((pair, qw, tokens), lambda h, s: (h, 0, 0)),
            scratch_shapes=[pltpu.VMEM((width, span), BF16)],
        ),
        compiler_params=pltpu.CompilerParams(vmem_limit_bytes=24 << 20),
        cost_estimate=pl.CostEstimate(
            flops=2 * heads * tokens * (span * width + latw * nope),
            transcendentals=0, bytes_accessed=8 << 20,
        ),
        name="query_gradient",
    )(info, ds, w_uk, own, *mine, *theirs)


def along_seq(distance, crossings=True):
    devices = lax.axis_size("seq")
    pairs = []
    for source in range(devices):
        target = source + distance
        if 0 <= target < devices:
            crossing = (2 * source < devices) != (2 * target < devices)
            if crossings or not crossing:
                pairs += between(source, target, crossing)
    return pairs


def between(source, target, turned=False):
    heads = lax.axis_size("head")
    pairs = []
    for head in range(heads):
        chip, core = divmod(head, CORES)
        if turned:
            chip ^= heads // CORES // 2
        pairs.append((source * heads + head, target * heads + chip * CORES + core))
    return pairs


def send(value, pairs):
    return lax.ppermute(value, ("seq", "head"), pairs)


def in_hbm(value):
    return pltpu.with_memory_space_constraint(value, pltpu.HBM)


def swap_cores(value):
    return lax.ppermute(value, "head", [(k, k ^ 1) for k in range(lax.axis_size("head"))])


def shards(queries, grad_out, latent, w_uk, w_uv, doc_start):
    tokens, width = latent.shape
    factor = queries.shape[2] ** (-0.5)
    seq, head = lax.axis_index("seq"), lax.axis_index("head")
    heads = lax.axis_size("head")
    chips = heads // CORES
    core, chip = head % CORES, head // CORES
    half = width // CORES

    own = latent.T
    part = jnp.where(core == 0, own[:half], own[half:])
    far = send(part, along_seq(3))
    near = [send(part, along_seq(distance, False)) for distance in (2, 1)]

    middle = lax.axis_size("seq") // 2
    after, next_one, next_two = middle, middle + 1, middle + 2
    relays = (between(next_one, after) + between(next_two, next_one), between(next_two, after))

    info = jnp.stack([core, (seq - BACK) * tokens]).astype(jnp.int32)
    qt = jnp.transpose(queries, (1, 2, 0))
    gt = jnp.transpose(grad_out, (1, 2, 0))
    far, gt = lax.optimization_barrier((far, gt))
    relayed = [send(far, relay) for relay in relays]
    prepared = prepare(
        info, in_hbm(qt), gt, in_hbm(w_uk), in_hbm(w_uv), in_hbm(doc_start[None])
    )
    near, relayed, prepared = lax.optimization_barrier((near[::-1], relayed, prepared))
    qct, qc, glt, gl, bias = prepared
    mine = [far] + [direct + other for direct, other in zip(near[::-1], relayed)]
    theirs = [swap_cores(piece) for piece in mine]

    ds, keep, away = attend(
        info, doc_start, qct, glt, bias, own, mine, theirs, qc, gl, factor, chips
    )
    both = keep + swap_cores(away)
    far_kept, far_gone = halve(both[:BACK], 1, chip, 1)
    far_gone, ds = lax.optimization_barrier((far_gone, ds))
    arrived = trade(far_gone, 1)
    dq = query_gradient(info, in_hbm(ds), in_hbm(w_uk), own, mine, theirs, factor)
    arrived, dq, own_both = lax.optimization_barrier((arrived, dq, both[BACK:]))
    own_kept, own_gone = halve(own_both, 1, chip, 1)
    far = (far_kept.astype(F32) + arrived.astype(F32)).astype(BF16)
    back = [send(far[BACK - distance], along_seq(-distance)) for distance in range(1, BACK + 1)]
    back, own_arrived = lax.optimization_barrier((back, trade(own_gone, 1)))
    total = (own_kept.astype(F32) + own_arrived.astype(F32))[0]
    for piece in back:
        total = total + piece.astype(F32)
    bit = 2
    while bit < chips:
        kept, gone = halve(total, 0, chip, bit)
        total = kept + trade(gone.astype(BF16), bit).astype(F32)
        bit *= 2
    grad_query = jnp.transpose(dq, (2, 0, 1))
    return grad_query, total[0]


def halve(value, dim, chip, bit):
    lengths = value.shape
    halves = value.reshape(*lengths[:dim], lengths[dim] // 2, 2, *lengths[dim + 1 :])
    mine = chip // bit % 2
    return (
        lax.dynamic_index_in_dim(halves, mine, dim + 1, False),
        lax.dynamic_index_in_dim(halves, 1 - mine, dim + 1, False),
    )


def trade(value, bit):
    route = [(k, k ^ (bit * CORES)) for k in range(lax.axis_size("head"))]
    return lax.ppermute(value, "head", route)


def solution(mesh):
    placed = (
        P("seq", "head", None),
        P("seq", "head", None),
        P("seq", None),
        P("head", None, None),
        P("head", None, None),
        P("seq"),
    )
    return jax.shard_map(
        shards,
        mesh=mesh,
        in_specs=placed,
        out_specs=(P("seq", "head", None), P(("seq", "head"), None)),
        check_vma=False,
    )
```

```python
import functools
import math

import jax
import jax.numpy as jnp
from jax import lax
from jax.experimental import pallas as pl
from jax.experimental.pallas import tpu as pltpu
from jax.sharding import PartitionSpec as P

BACK = 3
CORES = 2
BF16 = jnp.bfloat16
F32 = jnp.float32


def dot(a, b, contract=((1,), (0,))):
    return lax.dot_general(a, b, (contract, ((), ())), preferred_element_type=F32)


LOWEST = -1e30
CHUNK = 64
PAIR = 1
LIMIT = 32


def prepare_kernel(
    info_ref, qt_ref, gt_ref, uk_ref, uv_ref, start_ref,
    qct_ref, qc_ref, glt_ref, gl_ref, bias_ref,
):
    pair, latw, nope = uk_ref.shape
    tokens = qt_ref.shape[2]
    for n in range(pair):
        uk, uv = uk_ref[n], uv_ref[n]
        rows = slice(n * tokens, (n + 1) * tokens)
        qct_ref[:latw, rows] = dot(uk, qt_ref[n, :nope]).astype(BF16)
        qct_ref[latw:, rows] = qt_ref[n, nope:]
        qc_ref[rows, :latw] = dot(qt_ref[n, :nope].T, uk, ((1,), (1,))).astype(BF16)
        qc_ref[rows, latw:] = qt_ref[n, nope:].T
        glt_ref[:, rows] = dot(uv, gt_ref[n]).astype(BF16)
        gl_ref[rows] = dot(gt_ref[n].T, uv, ((1,), (1,))).astype(BF16)
    shape = bias_ref.shape
    row = pl.program_id(0) * shape[0] + lax.broadcasted_iota(jnp.int32, shape, 0)
    kpos = info_ref[1] + row
    qpos = info_ref[1] + BACK * tokens + lax.broadcasted_iota(jnp.int32, shape, 1)
    visible = (kpos >= start_ref[...]) & (kpos <= qpos)
    bias_ref[...] = jnp.where(visible, 0.0, -jnp.inf).astype(F32)


def prepare(info, qt, gt, w_uk, w_uv, doc_start, pair=2):
    heads, qw, tokens = qt.shape
    latw, nope = w_uk.shape[1:]
    vdim = gt.shape[1]
    width = latw + qw - nope
    span = (BACK + 1) * tokens
    one = lambda *dims: pl.BlockSpec((pair, *dims), lambda h, s: (h, 0, 0))
    rows = lambda n, d: pl.BlockSpec((pair * n, d), lambda h, s: (h, 0))
    lanes = lambda d, n: pl.BlockSpec((d, pair * n), lambda h, s: (0, h))
    return pl.pallas_call(
        prepare_kernel,
        out_shape=(
            jax.ShapeDtypeStruct((width, heads * tokens), BF16),
            jax.ShapeDtypeStruct((heads * tokens, width), BF16),
            jax.ShapeDtypeStruct((latw, heads * tokens), BF16),
            jax.ShapeDtypeStruct((heads * tokens, latw), BF16),
            jax.ShapeDtypeStruct((span, tokens), F32),
        ),
        grid_spec=pltpu.PrefetchScalarGridSpec(
            num_scalar_prefetch=1,
            grid=(heads // pair,),
            in_specs=[
                one(qw, tokens), one(vdim, tokens), one(latw, nope), one(latw, vdim),
                pl.BlockSpec((1, tokens), lambda h, s: (0, 0)),
            ],
            out_specs=[
                lanes(width, tokens), rows(tokens, width), lanes(latw, tokens),
                rows(tokens, latw), rows(span // heads, tokens),
            ],
        ),
        compiler_params=pltpu.CompilerParams(vmem_limit_bytes=16 << 20),
        cost_estimate=pl.CostEstimate(
            flops=8 * heads * tokens * latw * nope, transcendentals=0,
            bytes_accessed=16 << 20,
        ),
        name="prepare",
    )(info, qt, gt, w_uk, w_uv, doc_start)


def join(block_ref, core, mine_ref, theirs_ref):
    rows = mine_ref.shape[0]
    block_ref[pl.ds(pl.multiple_of(core * rows, rows), rows)] = mine_ref[...]
    block_ref[pl.ds(pl.multiple_of((1 - core) * rows, rows), rows)] = theirs_ref[...]


def main_kernel(
    info_ref, start_ref, qct_ref, glt_ref, bias_ref, own_ref,
    m3_ref, m2_ref, m1_ref, t3_ref, t2_ref, t1_ref, qc_ref, gl_ref,
    ds_hbm, keep_ref, send_ref,
    block_s, keys_s, expo_s, dprob_s, p_s, ds_s, sems, *, factor, pair,
):
    core = info_ref[0]
    span, tokens = bias_ref.shape
    low = jnp.maximum(start_ref[0] - info_ref[1], 0) // tokens
    latw, queries = glt_ref.shape
    lanes = pair * tokens
    steps = queries // lanes
    chunk = CHUNK // pair
    scale = factor * math.log2(math.e)

    for block, (mine, theirs) in enumerate(
        ((m3_ref, t3_ref), (m2_ref, t2_ref), (m1_ref, t1_ref))
    ):
        join(block_s.at[block % 2], core, mine, theirs)
        keys_s[block * tokens : (block + 1) * tokens] = block_s[block % 2].T
    keys_s[BACK * tokens :] = own_ref[...].T

    def fold(x, op):
        return op(x.reshape(-1, 8, lanes), axis=0)

    def store_ds(step):
        lane = slice(step * lanes, (step + 1) * lanes)
        return pltpu.make_async_copy(ds_s.at[:, lane], ds_hbm.at[:, lane], sems.at[step])

    def heads_from(begin, step):
        lane = slice(step * lanes, (step + 1) * lanes)
        slot = step % 2
        tops, totals = [], []
        for block in range(begin, span, tokens):
            scores = dot(keys_s[block : block + tokens], qct_ref[:, lane])
            for c in range(0, tokens, chunk):
                at = slice(block + c, block + c + chunk)
                bias = jnp.concatenate([bias_ref[at]] * (lanes // tokens), 1)
                s = scores[c : c + chunk] * scale + bias
                top = jnp.max(fold(s, jnp.max), axis=0, keepdims=True)
                top = jnp.maximum(top, LOWEST)
                e = jnp.exp2(s - top)
                expo_s[slot, at] = e
                tops.append(top)
                totals.append(jnp.sum(fold(e, jnp.sum), axis=0, keepdims=True))
        top = functools.reduce(jnp.maximum, tops)
        weights = [jnp.exp2(t - top) for t in tops]
        inverse = 1.0 / sum(w * t for w, t in zip(weights, totals))
        delta = jnp.zeros((8, lanes), F32)
        for block in range(begin, span, tokens):
            dprob = dot(keys_s[block : block + tokens, :latw], glt_ref[:, lane])
            for c in range(0, tokens, chunk):
                at = slice(block + c, block + c + chunk)
                weight = weights[(block + c - begin) // chunk] * inverse
                p = (expo_s[slot, at] * weight).astype(BF16)
                dp = dprob[c : c + chunk]
                p_s[at, lane] = p
                dprob_s[slot, at] = dp
                delta = delta + fold(p.astype(F32) * dp, jnp.sum)
        delta = jnp.sum(delta, axis=0, keepdims=True)
        for c in range(begin, span, chunk):
            at = slice(c, c + chunk)
            ds = (p_s[at, lane].astype(F32) * (dprob_s[slot, at] - delta)).astype(BF16)
            ds_s[at, lane] = ds
        if begin:
            ds_s[:begin, lane] = jnp.zeros((begin, lanes), BF16)
        store_ds(step).start()

    def all_heads_from(begin):
        for step in range(steps):
            heads_from(begin, step)

    for block in range(BACK + 1):
        pl.when(low == block)(functools.partial(all_heads_from, block * tokens))
    groups, piece = keep_ref.shape[1:3]

    def gradient(block, _):
        at = pl.ds(pl.multiple_of(block * tokens, tokens), tokens)

        def put(column, value):
            sides = value.reshape(groups, CORES, piece, -1)
            zeroth, first = sides[:, 0], sides[:, 1]
            keep_ref[block, :, :, column] = jnp.where(core == 0, zeroth, first).astype(BF16)
            send_ref[block, :, :, column] = jnp.where(core == 0, first, zeroth).astype(BF16)

        key = dot(ds_s[at], qc_ref[...]) * factor
        put(slice(0, latw), key[:, :latw] + dot(p_s[at], gl_ref[...]))
        put(slice(latw, None), key[:, latw:])
        return 0

    def blank(block, _):
        keep_ref[block] = jnp.zeros(keep_ref.shape[1:], BF16)
        send_ref[block] = jnp.zeros(send_ref.shape[1:], BF16)
        return 0

    lax.fori_loop(0, low, blank, 0)
    lax.fori_loop(low, BACK + 1, gradient, 0)
    for step in range(steps):
        store_ds(step).wait()


def attend(info, doc_start, qct, glt, bias, own, mine, theirs, qc, gl, factor, groups, pair=PAIR):
    width, queries = qct.shape
    latw = glt.shape[0]
    span, tokens = bias.shape
    piece = tokens // CORES // groups
    out = (BACK + 1, groups, piece, width)
    scalars = pl.BlockSpec(memory_space=pltpu.SMEM)
    onchip = pl.BlockSpec(memory_space=pltpu.VMEM)
    operands = [qct, glt, bias, own, *mine, *theirs, qc, gl]
    return pl.pallas_call(
        functools.partial(main_kernel, factor=factor, pair=pair),
        out_shape=(
            pltpu.HBM((span, queries), BF16),
            jax.ShapeDtypeStruct(out, BF16),
            jax.ShapeDtypeStruct(out, BF16),
        ),
        in_specs=[scalars, scalars] + [onchip] * len(operands),
        out_specs=[pl.BlockSpec(memory_space=pl.ANY), onchip, onchip],
        scratch_shapes=[
            pltpu.VMEM((2, width, tokens), BF16),
            pltpu.VMEM((span, width), BF16),
            pltpu.VMEM((2, span, pair * tokens), F32),
            pltpu.VMEM((2, span, pair * tokens), F32),
            pltpu.VMEM((span, queries), BF16),
            pltpu.VMEM((span, queries), BF16),
            pltpu.SemaphoreType.DMA((queries // tokens // pair,)),
        ],
        compiler_params=pltpu.CompilerParams(vmem_limit_bytes=LIMIT << 20),
        cost_estimate=pl.CostEstimate(
            flops=4 * queries * span * (width + latw),
            transcendentals=queries * span, bytes_accessed=24 << 20,
        ),
        name="attend",
    )(info, doc_start, *operands)


def query_kernel(
    info_ref, ds_ref, uk_ref, own_ref, m3_ref, m2_ref, m1_ref, t3_ref, t2_ref, t1_ref,
    out_ref, keys_s, *, factor,
):
    core = info_ref[0]
    tokens = own_ref.shape[1]
    pair, latw, nope = uk_ref.shape

    @pl.when(pl.program_id(0) == 0)
    def _():
        for block, (mine, theirs) in enumerate(
            ((m3_ref, t3_ref), (m2_ref, t2_ref), (m1_ref, t1_ref))
        ):
            join(keys_s.at[:, pl.ds(block * tokens, tokens)], core, mine, theirs)
        keys_s[:, BACK * tokens :] = own_ref[...]

    all_dq = dot(keys_s[...], ds_ref[...]) * factor
    for n in range(pair):
        dq = all_dq[:, n * tokens : (n + 1) * tokens]
        dq_nope = dot(uk_ref[n], dq[:latw].astype(BF16), ((0,), (0,)))
        out_ref[n, :nope] = dq_nope.astype(BF16)
        out_ref[n, nope:] = dq[latw:].astype(BF16)


def query_gradient(info, ds, w_uk, own, mine, theirs, factor, pair=4):
    span = ds.shape[0]
    heads, latw, nope = w_uk.shape
    width, tokens = own.shape
    qw = nope + width - latw
    whole = lambda a: pl.BlockSpec(a.shape, lambda h, s: (0,) * a.ndim)
    return pl.pallas_call(
        functools.partial(query_kernel, factor=factor),
        out_shape=jax.ShapeDtypeStruct((heads, qw, tokens), BF16),
        grid_spec=pltpu.PrefetchScalarGridSpec(
            num_scalar_prefetch=1,
            grid=(heads // pair,),
            in_specs=[
                pl.BlockSpec((span, pair * tokens), lambda h, s: (0, h)),
                pl.BlockSpec((pair, latw, nope), lambda h, s: (h, 0, 0)),
                whole(own),
            ]
            + [whole(a) for a in (*mine, *theirs)],
            out_specs=pl.BlockSpec((pair, qw, tokens), lambda h, s: (h, 0, 0)),
            scratch_shapes=[pltpu.VMEM((width, span), BF16)],
        ),
        compiler_params=pltpu.CompilerParams(vmem_limit_bytes=24 << 20),
        cost_estimate=pl.CostEstimate(
            flops=2 * heads * tokens * (span * width + latw * nope),
            transcendentals=0, bytes_accessed=8 << 20,
        ),
        name="query_gradient",
    )(info, ds, w_uk, own, *mine, *theirs)


def along_seq(distance, crossings=True):
    devices = lax.axis_size("seq")
    pairs = []
    for source in range(devices):
        target = source + distance
        if 0 <= target < devices:
            crossing = (2 * source < devices) != (2 * target < devices)
            if crossings or not crossing:
                pairs += between(source, target, crossing)
    return pairs


def between(source, target, turned=False):
    heads = lax.axis_size("head")
    pairs = []
    for head in range(heads):
        chip, core = divmod(head, CORES)
        if turned:
            chip ^= heads // CORES // 2
        pairs.append((source * heads + head, target * heads + chip * CORES + core))
    return pairs


def send(value, pairs):
    return lax.ppermute(value, ("seq", "head"), pairs)


def in_hbm(value):
    return pltpu.with_memory_space_constraint(value, pltpu.HBM)


def swap_cores(value):
    return lax.ppermute(value, "head", [(k, k ^ 1) for k in range(lax.axis_size("head"))])


def shards(queries, grad_out, latent, w_uk, w_uv, doc_start):
    tokens, width = latent.shape
    factor = queries.shape[2] ** (-0.5)
    seq, head = lax.axis_index("seq"), lax.axis_index("head")
    heads = lax.axis_size("head")
    chips = heads // CORES
    core, chip = head % CORES, head // CORES
    half = width // CORES

    own = latent.T
    part = lax.dynamic_slice_in_dim(own, core * half, half, 0)
    far = send(part, along_seq(3))
    near = [send(part, along_seq(distance, False)) for distance in (2, 1)]

    middle = lax.axis_size("seq") // 2
    after, next_one, next_two = middle, middle + 1, middle + 2
    relays = (between(next_one, after) + between(next_two, next_one), between(next_two, after))

    info = jnp.stack([core, (seq - BACK) * tokens]).astype(jnp.int32)
    qt = jnp.transpose(queries, (1, 2, 0))
    gt = jnp.transpose(grad_out, (1, 2, 0))
    far, gt = lax.optimization_barrier((far, gt))
    relayed = [send(far, relay) for relay in relays]
    prepared = prepare(
        info, in_hbm(qt), gt, in_hbm(w_uk), in_hbm(w_uv), in_hbm(doc_start[None])
    )
    near, relayed, prepared = lax.optimization_barrier((near[::-1], relayed, prepared))
    qct, qc, glt, gl, bias = prepared
    mine = [far] + [direct + other for direct, other in zip(near[::-1], relayed)]
    theirs = [swap_cores(piece) for piece in mine]

    ds, keep, away = attend(
        info, doc_start, qct, glt, bias, own, mine, theirs, qc, gl, factor, chips
    )
    both = keep + swap_cores(away)
    far_kept, far_gone = halve(both[:BACK], 1, chip, 1)
    own_kept, own_gone = halve(both[BACK:], 1, chip, 1)
    far_gone, own_gone, ds = lax.optimization_barrier((far_gone, own_gone, ds))
    arrived = trade(far_gone, 1)
    dq = query_gradient(info, in_hbm(ds), in_hbm(w_uk), own, mine, theirs, factor)
    arrived, dq, own_gone = lax.optimization_barrier((arrived, dq, own_gone))
    far = (far_kept.astype(F32) + arrived.astype(F32)).astype(BF16)
    back = [send(far[BACK - distance], along_seq(-distance)) for distance in range(1, BACK + 1)]
    back, own_arrived = lax.optimization_barrier((back, trade(own_gone, 1)))
    total = (own_kept.astype(F32) + own_arrived.astype(F32))[0]
    for piece in back:
        total = total + piece.astype(F32)
    bit = 2
    while bit < chips:
        kept, gone = halve(total, 0, chip, bit)
        total = kept + trade(gone.astype(BF16), bit).astype(F32)
        bit *= 2
    grad_query = jnp.transpose(dq, (2, 0, 1))
    return grad_query, total[0]


def halve(value, dim, chip, bit):
    lengths = value.shape
    halves = value.reshape(*lengths[:dim], lengths[dim] // 2, 2, *lengths[dim + 1 :])
    mine = chip // bit % 2
    return (
        lax.dynamic_index_in_dim(halves, mine, dim + 1, False),
        lax.dynamic_index_in_dim(halves, 1 - mine, dim + 1, False),
    )


def trade(value, bit):
    route = [(k, k ^ (bit * CORES)) for k in range(lax.axis_size("head"))]
    return lax.ppermute(value, "head", route)


def solution(mesh):
    placed = (
        P("seq", "head", None),
        P("seq", "head", None),
        P("seq", None),
        P("head", None, None),
        P("head", None, None),
        P("seq"),
    )
    return jax.shard_map(
        shards,
        mesh=mesh,
        in_specs=placed,
        out_specs=(P("seq", "head", None), P(("seq", "head"), None)),
        check_vma=False,
    )
```

```python
import functools
import math

import jax
import jax.numpy as jnp
from jax import lax
from jax.experimental import pallas as pl
from jax.experimental.pallas import tpu as pltpu
from jax.sharding import PartitionSpec as P

BACK = 3
CORES = 2
BF16 = jnp.bfloat16
F32 = jnp.float32


def dot(a, b, contract=((1,), (0,))):
    return lax.dot_general(a, b, (contract, ((), ())), preferred_element_type=F32)


LOWEST = -1e30
CHUNK = 64
PAIR = 1
LIMIT = 32


def prepare_kernel(
    info_ref, qt_ref, gt_ref, uk_ref, uv_ref, start_ref,
    qct_ref, qc_ref, glt_ref, gl_ref, bias_ref,
):
    pair, latw, nope = uk_ref.shape
    tokens = qt_ref.shape[2]
    for n in range(pair):
        uk, uv = uk_ref[n], uv_ref[n]
        rows = slice(n * tokens, (n + 1) * tokens)
        qct_ref[:latw, rows] = dot(uk, qt_ref[n, :nope]).astype(BF16)
        qct_ref[latw:, rows] = qt_ref[n, nope:]
        qc_ref[rows, :latw] = dot(qt_ref[n, :nope].T, uk, ((1,), (1,))).astype(BF16)
        qc_ref[rows, latw:] = qt_ref[n, nope:].T
        glt_ref[:, rows] = dot(uv, gt_ref[n]).astype(BF16)
        gl_ref[rows] = dot(gt_ref[n].T, uv, ((1,), (1,))).astype(BF16)
    shape = bias_ref.shape
    row = pl.program_id(0) * shape[0] + lax.broadcasted_iota(jnp.int32, shape, 0)
    kpos = info_ref[1] + row
    qpos = info_ref[1] + BACK * tokens + lax.broadcasted_iota(jnp.int32, shape, 1)
    visible = (kpos >= start_ref[...]) & (kpos <= qpos)
    bias_ref[...] = jnp.where(visible, 0.0, -jnp.inf).astype(F32)


def prepare(info, qt, gt, w_uk, w_uv, doc_start, pair=2):
    heads, qw, tokens = qt.shape
    latw, nope = w_uk.shape[1:]
    vdim = gt.shape[1]
    width = latw + qw - nope
    span = (BACK + 1) * tokens
    one = lambda *dims: pl.BlockSpec((pair, *dims), lambda h, s: (h, 0, 0))
    rows = lambda n, d: pl.BlockSpec((pair * n, d), lambda h, s: (h, 0))
    lanes = lambda d, n: pl.BlockSpec((d, pair * n), lambda h, s: (0, h))
    return pl.pallas_call(
        prepare_kernel,
        out_shape=(
            jax.ShapeDtypeStruct((width, heads * tokens), BF16),
            jax.ShapeDtypeStruct((heads * tokens, width), BF16),
            jax.ShapeDtypeStruct((latw, heads * tokens), BF16),
            jax.ShapeDtypeStruct((heads * tokens, latw), BF16),
            jax.ShapeDtypeStruct((span, tokens), F32),
        ),
        grid_spec=pltpu.PrefetchScalarGridSpec(
            num_scalar_prefetch=1,
            grid=(heads // pair,),
            in_specs=[
                one(qw, tokens), one(vdim, tokens), one(latw, nope), one(latw, vdim),
                pl.BlockSpec((1, tokens), lambda h, s: (0, 0)),
            ],
            out_specs=[
                lanes(width, tokens), rows(tokens, width), lanes(latw, tokens),
                rows(tokens, latw), rows(span // heads, tokens),
            ],
        ),
        compiler_params=pltpu.CompilerParams(vmem_limit_bytes=16 << 20),
        cost_estimate=pl.CostEstimate(
            flops=8 * heads * tokens * latw * nope, transcendentals=0,
            bytes_accessed=16 << 20,
        ),
        name="prepare",
    )(info, qt, gt, w_uk, w_uv, doc_start)


def join(block_ref, core, mine_ref, theirs_ref):
    rows = mine_ref.shape[0]
    block_ref[pl.ds(pl.multiple_of(core * rows, rows), rows)] = mine_ref[...]
    block_ref[pl.ds(pl.multiple_of((1 - core) * rows, rows), rows)] = theirs_ref[...]


def main_kernel(
    info_ref, start_ref, qct_ref, glt_ref, bias_ref, own_ref,
    m3_ref, m2_ref, m1_ref, t3_ref, t2_ref, t1_ref, qc_ref, gl_ref,
    ds_hbm, keep_ref, send_ref,
    block_s, keys_s, expo_s, dprob_s, p_s, ds_s, sems, *, factor, pair,
):
    core, parity = info_ref[0], info_ref[2]
    span, tokens = bias_ref.shape
    low = jnp.maximum(start_ref[0] - info_ref[1], 0) // tokens
    latw, queries = glt_ref.shape
    lanes = pair * tokens
    steps = queries // lanes
    chunk = CHUNK // pair
    scale = factor * math.log2(math.e)

    for block, (mine, theirs) in enumerate(
        ((m3_ref, t3_ref), (m2_ref, t2_ref), (m1_ref, t1_ref))
    ):
        join(block_s.at[block % 2], core, mine, theirs)
        keys_s[block * tokens : (block + 1) * tokens] = block_s[block % 2].T
    keys_s[BACK * tokens :] = own_ref[...].T

    def fold(x, op):
        return op(x.reshape(-1, 8, lanes), axis=0)

    def store_ds(step):
        lane = slice(step * lanes, (step + 1) * lanes)
        return pltpu.make_async_copy(ds_s.at[:, lane], ds_hbm.at[:, lane], sems.at[step])

    def heads_from(begin, step):
        lane = slice(step * lanes, (step + 1) * lanes)
        slot = step % 2
        tops, totals = [], []
        for block in range(begin, span, tokens):
            scores = dot(keys_s[block : block + tokens], qct_ref[:, lane])
            for c in range(0, tokens, chunk):
                at = slice(block + c, block + c + chunk)
                bias = jnp.concatenate([bias_ref[at]] * (lanes // tokens), 1)
                s = scores[c : c + chunk] * scale + bias
                top = jnp.max(fold(s, jnp.max), axis=0, keepdims=True)
                top = jnp.maximum(top, LOWEST)
                e = jnp.exp2(s - top)
                expo_s[slot, at] = e
                tops.append(top)
                totals.append(jnp.sum(fold(e, jnp.sum), axis=0, keepdims=True))
        top = functools.reduce(jnp.maximum, tops)
        weights = [jnp.exp2(t - top) for t in tops]
        inverse = 1.0 / sum(w * t for w, t in zip(weights, totals))
        delta = jnp.zeros((8, lanes), F32)
        for block in range(begin, span, tokens):
            dprob = dot(keys_s[block : block + tokens, :latw], glt_ref[:, lane])
            for c in range(0, tokens, chunk):
                at = slice(block + c, block + c + chunk)
                weight = weights[(block + c - begin) // chunk] * inverse
                p = (expo_s[slot, at] * weight).astype(BF16)
                dp = dprob[c : c + chunk]
                p_s[at, lane] = p
                dprob_s[slot, at] = dp
                delta = delta + fold(p.astype(F32) * dp, jnp.sum)
        delta = jnp.sum(delta, axis=0, keepdims=True)
        for c in range(begin, span, chunk):
            at = slice(c, c + chunk)
            ds = (p_s[at, lane].astype(F32) * (dprob_s[slot, at] - delta)).astype(BF16)
            ds_s[at, lane] = ds
        if begin:
            ds_s[:begin, lane] = jnp.zeros((begin, lanes), BF16)
        store_ds(step).start()

    def all_heads_from(begin):
        for step in range(steps):
            heads_from(begin, step)

    for block in range(BACK + 1):
        pl.when(low == block)(functools.partial(all_heads_from, block * tokens))
    groups, piece = keep_ref.shape[2:4]

    def gradient(block, _):
        at = pl.ds(pl.multiple_of(block * tokens, tokens), tokens)

        def put(column, value):
            sides = value.astype(BF16).reshape(groups, 2, CORES, piece, -1)
            zeroth, first = sides[:, :, 0], sides[:, :, 1]
            for ref, rows in (
                (keep_ref, jnp.where(core == 0, zeroth, first)),
                (send_ref, jnp.where(core == 0, first, zeroth)),
            ):
                even, odd = rows[:, 0], rows[:, 1]
                ref[0, block, :, :, column] = jnp.where(parity == 0, even, odd)
                ref[1, block, :, :, column] = jnp.where(parity == 0, odd, even)

        key = dot(ds_s[at], qc_ref[...]) * factor
        put(slice(0, latw), key[:, :latw] + dot(p_s[at], gl_ref[...]))
        put(slice(latw, None), key[:, latw:])
        return 0

    def blank(block, _):
        keep_ref[:, block] = jnp.zeros((2, groups, piece, keep_ref.shape[4]), BF16)
        send_ref[:, block] = jnp.zeros((2, groups, piece, send_ref.shape[4]), BF16)
        return 0

    lax.fori_loop(0, low, blank, 0)
    lax.fori_loop(low, BACK + 1, gradient, 0)
    for step in range(steps):
        store_ds(step).wait()


def attend(info, doc_start, qct, glt, bias, own, mine, theirs, qc, gl, factor, groups, pair=PAIR):
    width, queries = qct.shape
    latw = glt.shape[0]
    span, tokens = bias.shape
    piece = tokens // CORES // groups
    out = (2, BACK + 1, groups // 2, piece, width)
    scalars = pl.BlockSpec(memory_space=pltpu.SMEM)
    onchip = pl.BlockSpec(memory_space=pltpu.VMEM)
    operands = [qct, glt, bias, own, *mine, *theirs, qc, gl]
    return pl.pallas_call(
        functools.partial(main_kernel, factor=factor, pair=pair),
        out_shape=(
            pltpu.HBM((span, queries), BF16),
            jax.ShapeDtypeStruct(out, BF16),
            jax.ShapeDtypeStruct(out, BF16),
        ),
        in_specs=[scalars, scalars] + [onchip] * len(operands),
        out_specs=[pl.BlockSpec(memory_space=pl.ANY), onchip, onchip],
        scratch_shapes=[
            pltpu.VMEM((2, width, tokens), BF16),
            pltpu.VMEM((span, width), BF16),
            pltpu.VMEM((2, span, pair * tokens), F32),
            pltpu.VMEM((2, span, pair * tokens), F32),
            pltpu.VMEM((span, queries), BF16),
            pltpu.VMEM((span, queries), BF16),
            pltpu.SemaphoreType.DMA((queries // tokens // pair,)),
        ],
        compiler_params=pltpu.CompilerParams(vmem_limit_bytes=LIMIT << 20),
        cost_estimate=pl.CostEstimate(
            flops=4 * queries * span * (width + latw),
            transcendentals=queries * span, bytes_accessed=24 << 20,
        ),
        name="attend",
    )(info, doc_start, *operands)


def query_kernel(
    info_ref, ds_ref, uk_ref, own_ref, m3_ref, m2_ref, m1_ref, t3_ref, t2_ref, t1_ref,
    out_ref, keys_s, *, factor,
):
    core = info_ref[0]
    tokens = own_ref.shape[1]
    pair, latw, nope = uk_ref.shape

    @pl.when(pl.program_id(0) == 0)
    def _():
        for block, (mine, theirs) in enumerate(
            ((m3_ref, t3_ref), (m2_ref, t2_ref), (m1_ref, t1_ref))
        ):
            join(keys_s.at[:, pl.ds(block * tokens, tokens)], core, mine, theirs)
        keys_s[:, BACK * tokens :] = own_ref[...]

    all_dq = dot(keys_s[...], ds_ref[...]) * factor
    for n in range(pair):
        dq = all_dq[:, n * tokens : (n + 1) * tokens]
        dq_nope = dot(uk_ref[n], dq[:latw].astype(BF16), ((0,), (0,)))
        out_ref[n, :nope] = dq_nope.astype(BF16)
        out_ref[n, nope:] = dq[latw:].astype(BF16)


def query_gradient(info, ds, w_uk, own, mine, theirs, factor, pair=4):
    span = ds.shape[0]
    heads, latw, nope = w_uk.shape
    width, tokens = own.shape
    qw = nope + width - latw
    whole = lambda a: pl.BlockSpec(a.shape, lambda h, s: (0,) * a.ndim)
    return pl.pallas_call(
        functools.partial(query_kernel, factor=factor),
        out_shape=jax.ShapeDtypeStruct((heads, qw, tokens), BF16),
        grid_spec=pltpu.PrefetchScalarGridSpec(
            num_scalar_prefetch=1,
            grid=(heads // pair,),
            in_specs=[
                pl.BlockSpec((span, pair * tokens), lambda h, s: (0, h)),
                pl.BlockSpec((pair, latw, nope), lambda h, s: (h, 0, 0)),
                whole(own),
            ]
            + [whole(a) for a in (*mine, *theirs)],
            out_specs=pl.BlockSpec((pair, qw, tokens), lambda h, s: (h, 0, 0)),
            scratch_shapes=[pltpu.VMEM((width, span), BF16)],
        ),
        compiler_params=pltpu.CompilerParams(vmem_limit_bytes=24 << 20),
        cost_estimate=pl.CostEstimate(
            flops=2 * heads * tokens * (span * width + latw * nope),
            transcendentals=0, bytes_accessed=8 << 20,
        ),
        name="query_gradient",
    )(info, ds, w_uk, own, *mine, *theirs)


def along_seq(distance, crossings=True):
    devices = lax.axis_size("seq")
    pairs = []
    for source in range(devices):
        target = source + distance
        if 0 <= target < devices:
            crossing = (2 * source < devices) != (2 * target < devices)
            if crossings or not crossing:
                pairs += between(source, target, crossing)
    return pairs


def between(source, target, turned=False):
    heads = lax.axis_size("head")
    pairs = []
    for head in range(heads):
        chip, core = divmod(head, CORES)
        if turned:
            chip ^= heads // CORES // 2
        pairs.append((source * heads + head, target * heads + chip * CORES + core))
    return pairs


def send(value, pairs):
    return lax.ppermute(value, ("seq", "head"), pairs)


def in_hbm(value):
    return pltpu.with_memory_space_constraint(value, pltpu.HBM)


def swap_cores(value):
    return lax.ppermute(value, "head", [(k, k ^ 1) for k in range(lax.axis_size("head"))])


def shards(queries, grad_out, latent, w_uk, w_uv, doc_start):
    tokens, width = latent.shape
    factor = queries.shape[2] ** (-0.5)
    seq, head = lax.axis_index("seq"), lax.axis_index("head")
    heads = lax.axis_size("head")
    chips = heads // CORES
    core, chip = head % CORES, head // CORES
    half = width // CORES

    own = latent.T
    part = lax.dynamic_slice_in_dim(own, core * half, half, 0)
    far = send(part, along_seq(3))
    near = [send(part, along_seq(distance, False)) for distance in (2, 1)]

    middle = lax.axis_size("seq") // 2
    after, next_one, next_two = middle, middle + 1, middle + 2
    relays = (between(next_one, after) + between(next_two, next_one), between(next_two, after))

    info = jnp.stack([core, (seq - BACK) * tokens, chip % 2]).astype(jnp.int32)
    qt = jnp.transpose(queries, (1, 2, 0))
    gt = jnp.transpose(grad_out, (1, 2, 0))
    far, gt = lax.optimization_barrier((far, gt))
    relayed = [send(far, relay) for relay in relays]
    prepared = prepare(
        info, in_hbm(qt), gt, in_hbm(w_uk), in_hbm(w_uv), in_hbm(doc_start[None])
    )
    near, relayed, prepared = lax.optimization_barrier((near[::-1], relayed, prepared))
    qct, qc, glt, gl, bias = prepared
    mine = [far] + [direct + other for direct, other in zip(near[::-1], relayed)]
    theirs = [swap_cores(piece) for piece in mine]

    ds, keep, away = attend(
        info, doc_start, qct, glt, bias, own, mine, theirs, qc, gl, factor, chips
    )
    swapped = swap_cores(away)
    far_gone = keep[1, :BACK] + swapped[1, :BACK]
    own_gone = keep[1, BACK] + swapped[1, BACK]
    far_gone, own_gone, ds = lax.optimization_barrier((far_gone, own_gone, ds))
    arrived = trade(far_gone, 1)
    dq = query_gradient(info, in_hbm(ds), in_hbm(w_uk), own, mine, theirs, factor)
    arrived, dq, own_gone = lax.optimization_barrier((arrived, dq, own_gone))
    kept = keep[0].astype(F32) + swapped[0].astype(F32)
    far = (kept[:BACK] + arrived.astype(F32)).astype(BF16)
    far, own_gone = lax.optimization_barrier((far, own_gone))
    back = [send(far[BACK - distance], along_seq(-distance)) for distance in range(1, BACK + 1)]
    back, own_arrived = lax.optimization_barrier((back, trade(own_gone, 1)))
    total = kept[BACK] + own_arrived.astype(F32)
    for piece in back:
        total = total + piece.astype(F32)
    bit = 2
    while bit < chips:
        kept, gone = halve(total, 0, chip, bit)
        total = kept + trade(gone.astype(BF16), bit).astype(F32)
        bit *= 2
    grad_query = jnp.transpose(dq, (2, 0, 1))
    return grad_query, total[0]


def halve(value, dim, chip, bit):
    lengths = value.shape
    halves = value.reshape(*lengths[:dim], lengths[dim] // 2, 2, *lengths[dim + 1 :])
    mine = chip // bit % 2
    return (
        lax.dynamic_index_in_dim(halves, mine, dim + 1, False),
        lax.dynamic_index_in_dim(halves, 1 - mine, dim + 1, False),
    )


def trade(value, bit):
    route = [(k, k ^ (bit * CORES)) for k in range(lax.axis_size("head"))]
    return lax.ppermute(value, "head", route)


def solution(mesh):
    placed = (
        P("seq", "head", None),
        P("seq", "head", None),
        P("seq", None),
        P("head", None, None),
        P("head", None, None),
        P("seq"),
    )
    return jax.shard_map(
        shards,
        mesh=mesh,
        in_specs=placed,
        out_specs=(P("seq", "head", None), P(("seq", "head"), None)),
        check_vma=False,
    )
```
